512 devices in a mesh: req: 64 (over y, z_lo, core), head: 8 (over z_hi, x).
Axes of the slice: x: 4, y: 8, z: 8 (z_hi: 2, z_lo: 4; z = z_hi * 4 + z_lo), core: 2. Of those that a mesh axis runs over, the one named last changes fastest.
Arguments:
- queries: bfloat16 [256, 8192], P('req', 'head'), may hold values from -200 to 200
- new_kv: bfloat16 [2, 256, 1024], P(None, 'req', 'head'), may hold values from -6 to 6
- own_kv: bfloat16 [2, 2048, 64, 1024], P(None, 'req', None, 'head'), may hold values from -6 to 6
- man_kv: bfloat16 [2, 128, 64, 1024], P(None, 'req', None, 'head'), may hold values from -6 to 6
- pages: int32 [256, 8], P('req'), may hold values from 0 to 31
- own_len: int32 [256], P('req'), may hold values from 1 to 8, as said below
- resid: bfloat16 [256, 8192], P(None, 'req'), may hold values from -3 to 3
- w_out: bfloat16 [8192, 8192], P('head', 'req'), may hold values from -0.8984375 to 0.8984375
- w_gate: bfloat16 [8192, 14336], P('req', 'head'), may hold values from -0.0625 to 0.0625
- w_up: bfloat16 [8192, 14336], P('req', 'head'), may hold values from -0.0625 to 0.0625
Outputs:
- resid_out: bfloat16 [256, 8192], P(None, 'req')
- hidden: bfloat16 [256, 14336], P('req', 'head')
The draws below stay inside these ranges and needn't reach their ends.
Inputs may be any that keep to these rules, and one draw needn't show every extreme that they name: `pages`: entries at and past a request's length are padding. `own_len`: among the 4 requests of each index of req one has 8 pages.
All inputs are finite; a program needn't handle non-finite values.
Results may differ from the reference program's by a relative error of at most 0.03.
Values may be sent and summed in bfloat16 or wider, within the bound.
No kernel may reach another device: no remote copies, remote signals or barrier semaphores. Data moves between devices by JAX's collectives and lax.ppermute only.
A program may use at most 64 MiB of HBM per device.

```python
import jax
import jax.numpy as jnp
from jax import lax

D = 8192
HEADS = 64
KVH = 8
HD = 128
FF = 14336
PAGE = 64
MAXP = 8
REQ_DEV = 4
GROUP = 8
POOL_DEV = 32
REQS = 256
MANP = 128
N_REQ = 64


def draw_queries(key, part):
    base = jax.random.normal(key, (REQS, HEADS * HD), jnp.float32) * 1.5
    return jnp.clip(base, -200.0, 200.0).astype(jnp.bfloat16)


def draw_own_len(key, part):
    blocks = REQS // REQ_DEV
    lengths = jax.random.randint(key, (REQS,), 1, MAXP + 1)
    chosen = jax.random.randint(jax.random.fold_in(key, 5), (blocks,), 0, REQ_DEV)
    where = jnp.arange(blocks, dtype=jnp.int32) * REQ_DEV + chosen
    return lengths.at[where].set(MAXP).astype(jnp.int32)


def place_ends(array, stream_key, low, top_value):
    longest = array.shape.index(max(array.shape))
    spots = []
    for shift in (0, 1):
        where = [jax.random.randint(jax.random.fold_in(stream_key, axis), (), 0, length) for axis, length in enumerate(array.shape)]
        where[longest] = (where[longest] + shift) % array.shape[longest]
        spots.append(tuple(where))
    return array.at[spots[0]].set(low).at[spots[1]].set(top_value)


def level_of(rng, extent, cuts, smallest, high):
    gain = 1.0
    for dim, parts in cuts:
        heights = jax.random.uniform(jax.random.fold_in(jax.random.fold_in(rng, 6), dim), (parts,), jnp.float32, smallest / len(cuts), high / len(cuts))
        gain = gain * jnp.repeat(jnp.exp(heights), extent[dim] // parts).reshape((-1,) + (1,) * (len(extent) - 1 - dim))
    return gain


def normal_values(stream_key, dims, scale, bound, split=(), held_as=jnp.bfloat16):
    array = jax.random.normal(stream_key, dims, jnp.float32) * scale
    if len(split) > 0:
        array = level_of(stream_key, dims, split, -0.22, 0.18) * array
    return jnp.clip(array, min=-bound, max=bound).astype(held_as)


def setup_inputs(seed: int = 0) -> dict:
    arg_keys = jax.random.split(jax.random.key(seed), 11)
    queries = draw_queries(jax.random.fold_in(arg_keys[10], 71), 0)
    new_kv = normal_values(arg_keys[1], (2, REQS, KVH * HD), 1.0, 6.0, ((1, 64), (2, 8)))
    own_kv = normal_values(arg_keys[2], (2, POOL_DEV * N_REQ, PAGE, KVH * HD), 1.0, 6.0, ((1, 64), (3, 8)))
    man_kv = normal_values(arg_keys[3], (2, MANP, PAGE, KVH * HD), 1.0, 6.0, ((1, 64), (3, 8)))
    pages = place_ends(jax.random.randint(arg_keys[4], (REQS, MAXP), 0, POOL_DEV), jax.random.fold_in(arg_keys[4], 1), 0, POOL_DEV - 1).astype(jnp.int32)
    own_len = draw_own_len(jax.random.fold_in(arg_keys[10], 71), 0)
    resid = normal_values(arg_keys[6], (REQS, D), 0.5, 3.0, ((1, 64),))
    w_out = normal_values(arg_keys[7], (HEADS * HD, D), 0.15, 0.8984375, ((0, 8), (1, 64)))
    w_gate = normal_values(arg_keys[8], (D, FF), D ** -0.5, 0.0625, ((0, 64), (1, 8)))
    w_up = normal_values(arg_keys[9], (D, FF), D ** -0.5, 0.0625, ((0, 64), (1, 8)))
    return dict(queries=queries, new_kv=new_kv, own_kv=own_kv, man_kv=man_kv, pages=pages, own_len=own_len, resid=resid, w_out=w_out, w_gate=w_gate, w_up=w_up)


def reference(queries, new_kv, own_kv, man_kv, pages, own_len, resid, w_out, w_gate, w_up):
    scale = HD ** -0.5
    q_all = queries.reshape(REQS, KVH, GROUP, HD)
    owner = (jnp.arange(REQS, dtype=jnp.int32) // REQ_DEV) * POOL_DEV
    global_pages = (owner[:, None] + pages).astype(jnp.int32)
    valid = jnp.arange(MAXP, dtype=jnp.int32)[None, :] < own_len[:, None]
    valid = jnp.repeat(valid, PAGE, axis=1)
    own_heads = own_kv.reshape(2, POOL_DEV * N_REQ, PAGE, KVH, HD)
    man_heads = man_kv.reshape(2, MANP * PAGE, KVH, HD)
    new_heads = new_kv.reshape(2, REQS, KVH, HD)

    def one_head(index):
        q_head = lax.dynamic_index_in_dim(q_all, index, 1, keepdims=False).astype(jnp.float32)
        man_k = lax.dynamic_index_in_dim(man_heads[0], index, 1, keepdims=False).astype(jnp.float32)
        man_v = lax.dynamic_index_in_dim(man_heads[1], index, 1, keepdims=False).astype(jnp.float32)
        pool_k = lax.dynamic_index_in_dim(own_heads[0], index, 2, keepdims=False)
        pool_v = lax.dynamic_index_in_dim(own_heads[1], index, 2, keepdims=False)
        own_k = pool_k[global_pages].reshape(REQS, MAXP * PAGE, HD).astype(jnp.float32)
        own_v = pool_v[global_pages].reshape(REQS, MAXP * PAGE, HD).astype(jnp.float32)
        new_k = lax.dynamic_index_in_dim(new_heads[0], index, 1, keepdims=False).astype(jnp.float32)
        new_v = lax.dynamic_index_in_dim(new_heads[1], index, 1, keepdims=False).astype(jnp.float32)
        s_man = jnp.einsum('bgd,td->bgt', q_head, man_k) * scale
        s_own = jnp.einsum('bgd,btd->bgt', q_head, own_k) * scale
        s_own = jnp.where(valid[:, None, :], s_own, -jnp.inf)
        s_new = jnp.einsum('bgd,bd->bg', q_head, new_k) * scale
        top = jnp.maximum(jnp.maximum(s_man.max(-1), s_own.max(-1)), s_new)
        p_man = jnp.exp(s_man - top[..., None])
        p_own = jnp.exp(s_own - top[..., None])
        p_new = jnp.exp(s_new - top)
        total = p_man.sum(-1) + p_own.sum(-1) + p_new
        b_man = p_man.astype(jnp.bfloat16).astype(jnp.float32)
        b_own = p_own.astype(jnp.bfloat16).astype(jnp.float32)
        b_new = p_new.astype(jnp.bfloat16).astype(jnp.float32)
        acc = jnp.einsum('bgt,td->bgd', b_man, man_v) + jnp.einsum('bgt,btd->bgd', b_own, own_v)
        acc = acc + b_new[..., None] * new_v[:, None, :]
        return (acc / total[..., None]).astype(jnp.bfloat16)

    head_split = lax.map(one_head, jnp.arange(KVH, dtype=jnp.int32))
    attn = jnp.transpose(head_split, (1, 0, 2, 3)).reshape(REQS, HEADS * HD)
    projected_rows = jnp.dot(attn, w_out, preferred_element_type=jnp.float32)
    resid_out = (resid.astype(jnp.float32) + projected_rows).astype(jnp.bfloat16)
    gate = jnp.dot(resid_out, w_gate, preferred_element_type=jnp.float32)
    up = jnp.dot(resid_out, w_up, preferred_element_type=jnp.float32)
    hidden = (jax.nn.silu(gate) * up).astype(jnp.bfloat16)
    return resid_out, hidden
```

```python
import jax
import jax.numpy as jnp
from jax import lax
from jax.experimental import pallas as pl
from jax.experimental.pallas import tpu as pltpu
from jax.sharding import Mesh, PartitionSpec as P

HD = 128
PAGE = 64
MAXP = 8
GROUP = 8
ROWS = 4
QROWS = ROWS * GROUP
POOL = 32
CHIPS = 32
STATS = 8
SCALE = HD**-0.5
PLANE = ("y", "zl")
HEAD = ("zh", "x")
REQ = ("y", "zl", "c")
BF = jnp.bfloat16
F32 = jnp.float32


def dot(a, b, ca, cb):
    return lax.dot_general(a, b, (((ca,), (cb,)), ((), ())), preferred_element_type=F32)


def own_kernel(pages_ref, len_ref, q_ref, new_ref, own_ref, acc_ref, top_ref, total_ref):
    tokens = POOL * PAGE
    scores = dot(q_ref[...], own_ref[0], 1, 1) * SCALE
    page_of = lax.broadcasted_iota(jnp.int32, (GROUP, tokens), 1) // PAGE
    weights, tops, totals, news = [], [], [], []
    for b in range(ROWS):
        count = jnp.zeros((GROUP, tokens), F32)
        for i in range(MAXP):
            page = jnp.where(i < len_ref[b], pages_ref[b, i], -1)
            count = count + jnp.where(page_of == page, 1.0, 0.0)
        s = jnp.where(count > 0.0, scores[b * GROUP : (b + 1) * GROUP], -jnp.inf)
        q = q_ref[b * GROUP : (b + 1) * GROUP].astype(F32)
        s_new = jnp.sum(q * new_ref[0, b : b + 1].astype(F32), axis=1, keepdims=True) * SCALE
        top = jnp.maximum(jnp.max(s, axis=1, keepdims=True), s_new)
        w = jnp.exp(s - top) * count
        w_new = jnp.exp(s_new - top)
        weights.append(w.astype(BF))
        tops.append(top)
        totals.append(jnp.sum(w, axis=1, keepdims=True) + w_new)
        news.append(w_new.astype(BF).astype(F32) * new_ref[1, b : b + 1].astype(F32))
    acc = dot(jnp.concatenate(weights, axis=0), own_ref[1], 1, 0)
    acc_ref[...] = acc + jnp.concatenate(news, axis=0)
    top_ref[...] = jnp.broadcast_to(jnp.concatenate(tops, axis=0), (QROWS, HD))
    total_ref[...] = jnp.broadcast_to(jnp.concatenate(totals, axis=0), (QROWS, HD))


def own_part(pages, own_len, q, new_kv, own_kv):
    smem = pl.BlockSpec(memory_space=pltpu.SMEM)
    vmem = pl.BlockSpec(memory_space=pltpu.VMEM)
    return pl.pallas_call(
        own_kernel,
        out_shape=[jax.ShapeDtypeStruct((QROWS, HD), F32)] * 3,
        in_specs=[smem, smem, vmem, vmem, vmem],
        out_specs=[vmem] * 3,
        compiler_params=pltpu.CompilerParams(vmem_limit_bytes=32 << 20),
        name="own_attention",
    )(pages, own_len, q, new_kv, own_kv)


def man_kernel(q_ref, kv_ref, out_ref):
    keys = jnp.concatenate([kv_ref[0, 0], kv_ref[1, 0]], axis=0)
    values = jnp.concatenate([kv_ref[0, 1], kv_ref[1, 1]], axis=0)
    row = lax.broadcasted_iota(jnp.int32, (STATS, HD), 0)
    for chunk in range(CHIPS * QROWS // HD):
        s = dot(keys, q_ref[chunk * HD : (chunk + 1) * HD], 1, 1) * SCALE
        top = jnp.max(s, axis=0, keepdims=True).astype(BF).astype(F32)
        w = jnp.exp(s - top)
        total = jnp.sum(w, axis=0, keepdims=True)
        high = total.astype(BF).astype(F32)
        acc = dot(w.astype(BF), values, 0, 0).astype(BF)
        stats = jnp.where(row == 0, top, jnp.where(row == 1, high, jnp.where(row == 2, total - high, 0.0)))
        stats = stats.astype(BF)
        for j in range(HD // QROWS):
            to = chunk * (HD // QROWS) + j
            out_ref[to, 0:QROWS] = acc[j * QROWS : (j + 1) * QROWS]
            out_ref[to, QROWS : QROWS + STATS] = stats


def man_part(q_all, kv):
    vmem = pl.BlockSpec(memory_space=pltpu.VMEM)
    return pl.pallas_call(
        man_kernel,
        out_shape=jax.ShapeDtypeStruct((CHIPS, QROWS + STATS, HD), BF),
        in_specs=[vmem, vmem],
        out_specs=vmem,
        compiler_params=pltpu.CompilerParams(vmem_limit_bytes=32 << 20),
        name="manifest_attention",
    )(q_all, kv)


def join_kernel(place_ref, parts_ref, acc_ref, top_ref, total_ref, out_ref, rows_ref):
    stats = parts_ref[:, QROWS : QROWS + STATS, :].reshape(CHIPS * STATS, HD)
    lane = lax.broadcasted_iota(jnp.int32, (QROWS, HD), 1)
    row = lax.broadcasted_iota(jnp.int32, (QROWS, HD), 0)
    pick = jnp.where(lane == row + place_ref[0] * QROWS, 1.0, 0.0).astype(BF)
    s = dot(pick, stats, 1, 1)
    n = CHIPS * STATS
    kind = lax.broadcasted_iota(jnp.int32, (QROWS, n), 1) % STATS
    totals = pltpu.roll(s, n - 1, 1) + pltpu.roll(s, n - 2, 1)
    own_top = top_ref[:, 0:1]
    top = jnp.maximum(jnp.max(jnp.where(kind == 0, s, -jnp.inf), axis=1, keepdims=True), own_top)
    factor = jnp.where(kind == 0, jnp.exp(jnp.minimum(s - top, 0.0)), 0.0)
    own_factor = jnp.exp(own_top - top)
    total = jnp.sum(factor * totals, axis=1, keepdims=True) + own_factor * total_ref[:, 0:1]
    acc = own_factor * acc_ref[...]
    for i in range(CHIPS):
        acc = acc + factor[:, i * STATS : i * STATS + 1] * parts_ref[i, 0:QROWS].astype(F32)
    rows_ref[...] = acc / total
    for h in range(GROUP):
        out_ref[:, h * HD : (h + 1) * HD] = rows_ref[pl.ds(h, ROWS, stride=GROUP), :].astype(BF)


def join_part(place, parts, acc, top, total):
    smem = pl.BlockSpec(memory_space=pltpu.SMEM)
    vmem = pl.BlockSpec(memory_space=pltpu.VMEM)
    return pl.pallas_call(
        join_kernel,
        out_shape=jax.ShapeDtypeStruct((ROWS, GROUP * HD), BF),
        in_specs=[smem, vmem, vmem, vmem, vmem],
        out_specs=vmem,
        scratch_shapes=[pltpu.VMEM((QROWS, HD), F32)],
        compiler_params=pltpu.CompilerParams(vmem_limit_bytes=32 << 20),
        name="join_attention",
    )(place, parts, acc, top, total)


def swap(x):
    return lax.ppermute(x, "c", [(0, 1), (1, 0)])


def spread(x, axes, n):
    return lax.all_to_all(jnp.broadcast_to(x[None], (n, *x.shape)), axes, 0, 0, tiled=True)


def on_device(queries, new_kv, own_kv, man_kv, pages, own_len, resid, w_out, w_gate, w_up):
    core = lax.axis_index("c")
    width = w_gate.shape[1]
    q = queries.reshape(QROWS, HD)
    kv = lax.all_gather(man_kv.reshape(2, 2 * PAGE, HD), "c", axis=0)
    w_out2 = jnp.concatenate([w_out, swap(w_out)], axis=1)
    w_gate2 = jnp.concatenate([w_gate, swap(w_gate)], axis=0)
    w_up2 = jnp.concatenate([w_up, swap(w_up)], axis=0)
    res = resid.reshape(CHIPS, 2, ROWS, HD)
    mine = jnp.where(core == 0, res[:, 0], res[:, 1])
    theirs = swap(jnp.where(core == 0, res[:, 1], res[:, 0]))
    res2 = jnp.concatenate([mine, theirs], axis=-1).reshape(CHIPS * ROWS, 2 * HD)

    acc, top, total = own_part(pages, own_len, q, new_kv, own_kv.reshape(2, POOL * PAGE, HD))
    q_all = spread(q, PLANE, CHIPS).reshape(CHIPS * QROWS, HD)
    parts = lax.all_to_all(man_part(q_all, kv), PLANE, 0, 0, tiled=True)
    place = lax.axis_index("zl").astype(jnp.int32).reshape(1)
    attn = join_part(place, parts, acc, top, total)
    attn_all = spread(attn, PLANE, CHIPS).reshape(CHIPS * ROWS, GROUP * HD)

    partial_out = jnp.dot(attn_all, w_out2, preferred_element_type=F32).astype(BF)
    summed = spread(partial_out, HEAD, 8).astype(F32).sum(0)
    out2 = (res2.astype(F32) + summed).astype(BF)

    gate_part = jnp.dot(out2, w_gate2, preferred_element_type=F32).astype(BF)
    up_part = jnp.dot(out2, w_up2, preferred_element_type=F32).astype(BF)
    both = jnp.concatenate(
        [gate_part.reshape(CHIPS, ROWS, width), up_part.reshape(CHIPS, ROWS, width)], axis=1
    )
    joined = lax.all_to_all(both, PLANE, 0, 0, tiled=True).astype(F32).sum(0)
    hidden = (jax.nn.silu(joined[:ROWS]) * joined[ROWS:]).astype(BF)

    kept = out2[:, :HD].reshape(CHIPS, 1, ROWS, HD)
    given = swap(out2[:, HD:]).reshape(CHIPS, 1, ROWS, HD)
    first = jnp.where(core == 0, kept, given)
    second = jnp.where(core == 0, given, kept)
    resid_out = jnp.concatenate([first, second], axis=1).reshape(CHIPS * 2 * ROWS, HD)
    return (resid_out, hidden)


def solution(mesh):
    fine = Mesh(mesh.devices.reshape(8, 4, 2, 2, 4), ("y", "zl", "c", "zh", "x"))
    in_specs = (
        P(REQ, HEAD),
        P(None, REQ, HEAD),
        P(None, REQ, None, HEAD),
        P(None, REQ, None, HEAD),
        P(REQ, None),
        P(REQ),
        P(None, REQ),
        P(HEAD, REQ),
        P(REQ, HEAD),
        P(REQ, HEAD),
    )
    out_specs = (P(None, REQ), P(REQ, HEAD))
    return jax.shard_map(
        on_device, mesh=fine, in_specs=in_specs, out_specs=out_specs, check_vma=False
    )
```

```python
import jax
import jax.numpy as jnp
from jax import lax
from jax.experimental import pallas as pl
from jax.experimental.pallas import tpu as pltpu
from jax.sharding import Mesh, PartitionSpec as P

HD = 128
PAGE = 64
MAXP = 8
GROUP = 8
ROWS = 4
QROWS = ROWS * GROUP
POOL = 32
NY = 8
NZ = 4
CHIPS = NY * NZ
SCALE = HD**-0.5
PLANE = ("y", "zl")
SIDE = ("zl", "zh", "x")
HEAD = ("zh", "x")
REQ = ("y", "zl", "c")
BF = jnp.bfloat16
F32 = jnp.float32
VMEM = pl.BlockSpec(memory_space=pltpu.VMEM)
SMEM = pl.BlockSpec(memory_space=pltpu.SMEM)


def dot(a, b, ca, cb):
    return lax.dot_general(a, b, (((ca,), (cb,)), ((), ())), preferred_element_type=F32)


def call(kernel, name, out_shape, *args, specs=None, scratch=()):
    return pl.pallas_call(
        kernel,
        out_shape=out_shape,
        in_specs=specs or [VMEM] * len(args),
        out_specs=jax.tree.map(lambda _: VMEM, out_shape),
        scratch_shapes=scratch,
        compiler_params=pltpu.CompilerParams(vmem_limit_bytes=40 << 20),
        name=name,
    )(*args)


def query_kernel(q_ref, out_ref, rows_ref):
    for h in range(GROUP):
        first = (h // 2) * 8 + h % 2
        rows_ref[pl.ds(first, ROWS, stride=2), :] = q_ref[:, h * HD : (h + 1) * HD].astype(F32)
    for z in range(NZ):
        block = rows_ref[z * 8 : z * 8 + 8].astype(BF)
        for y in range(NY):
            out_ref[y * NZ + z] = block


def own_kernel(pages_ref, len_ref, q_ref, new_ref, own_ref, out_ref):
    tokens = POOL * PAGE
    q = q_ref[0:NZ].reshape(QROWS, HD)
    scores = dot(q, own_ref[0], 1, 1) * SCALE
    page_of = lax.broadcasted_iota(jnp.int32, (8, tokens), 1) // PAGE
    req = lax.broadcasted_iota(jnp.int32, (8, HD), 0) // 2

    def by_request(values):
        return jnp.where(req == 0, values[0], jnp.where(req == 1, values[1], jnp.where(req == 2, values[2], values[3])))

    count = jnp.zeros((8, tokens), F32)
    for i in range(MAXP):
        page = by_request([jnp.where(i < len_ref[b], pages_ref[b, i], -1) for b in range(ROWS)])
        count = count + jnp.where(page_of == page[:, 0:1], 1.0, 0.0)
    new_k = by_request([new_ref[0, b : b + 1].astype(F32) for b in range(ROWS)])
    new_v = by_request([new_ref[1, b : b + 1].astype(F32) for b in range(ROWS)])
    lane = lax.broadcasted_iota(jnp.int32, (8, HD), 1)
    weights, news, stats = [], [], []
    for z in range(NZ):
        s = jnp.where(count > 0.0, scores[z * 8 : z * 8 + 8], -jnp.inf)
        s_new = jnp.sum(q_ref[z].astype(F32) * new_k, axis=1, keepdims=True) * SCALE
        top = jnp.maximum(jnp.max(s, axis=1, keepdims=True), s_new).astype(BF).astype(F32)
        w = jnp.exp(s - top) * count
        w_new = jnp.exp(s_new - top)
        total = jnp.sum(w, axis=1, keepdims=True) + w_new
        high = total.astype(BF).astype(F32)
        weights.append(w.astype(BF))
        news.append(w_new.astype(BF).astype(F32) * new_v)
        stats.append(jnp.where(lane == 0, top, jnp.where(lane == 1, high, jnp.where(lane == 2, total - high, 0.0))))
    acc = dot(jnp.concatenate(weights, axis=0), own_ref[1], 1, 0)
    for z in range(NZ):
        block = jnp.concatenate([acc[z * 8 : z * 8 + 8] + news[z], stats[z]], axis=0).astype(BF)
        for y in range(NY):
            out_ref[y * NZ + z] = block


def man_kernel(q_ref, kv_ref, out_ref):
    n = 2 * NZ
    keys = jnp.concatenate([kv_ref[i, 0] for i in range(n)], axis=0)
    values = jnp.concatenate([kv_ref[i, 1] for i in range(n)], axis=0)
    row = lax.broadcasted_iota(jnp.int32, (8, HD), 0)
    stats = jnp.zeros((8, HD), F32)
    accs = []
    for half in range(2):
        q = q_ref[half * 16 : half * 16 + 16].reshape(HD, HD)
        s = dot(keys, q, 1, 1) * SCALE
        top = jnp.max(s, axis=0, keepdims=True).astype(BF).astype(F32)
        w = jnp.exp(s - top)
        total = jnp.sum(w, axis=0, keepdims=True)
        high = total.astype(BF).astype(F32)
        accs.append(dot(w.astype(BF), values, 0, 0))
        for k, value in enumerate((top, high, total - high)):
            stats = jnp.where(row == 3 * half + k, value, stats)
    block = jnp.concatenate(accs + [stats], axis=0).astype(BF)
    for y in range(NY):
        out_ref[y] = block


def join_kernel(parts_ref, own_ref, w0_ref, w1_ref, out_ref, rows_ref):
    rows = 2 * HD
    stats = parts_ref[:, rows : rows + 8, :].reshape(NY * 8, HD)
    eye = lax.broadcasted_iota(jnp.int32, (HD, HD), 0) == lax.broadcasted_iota(jnp.int32, (HD, HD), 1)
    s = dot(jnp.where(eye, 1.0, 0.0).astype(BF), stats, 1, 1)
    n = NY * 8
    kind = lax.broadcasted_iota(jnp.int32, (HD, n), 1) % 8
    for half in range(2):
        base = 3 * half
        own = own_ref[half * 16 : half * 16 + 16].astype(F32)
        own_acc = own[:, 0:8].reshape(HD, HD)
        own_stats = own[:, 8:16].reshape(HD, HD)
        own_top = own_stats[:, 0:1]
        here = kind == base
        top = jnp.maximum(jnp.max(jnp.where(here, s, -jnp.inf), axis=1, keepdims=True), own_top)
        factor = jnp.where(here, jnp.exp(jnp.minimum(s - top, 0.0)), 0.0)
        totals = jnp.concatenate([s[:, 1:], s[:, :1]], axis=1) + jnp.concatenate([s[:, 2:], s[:, :2]], axis=1)
        own_factor = jnp.exp(own_top - top)
        total = jnp.sum(factor * totals, axis=1, keepdims=True) + own_factor * (own_stats[:, 1:2] + own_stats[:, 2:3])
        acc = own_factor * own_acc
        for y in range(NY):
            lane = y * 8 + base
            acc = acc + factor[:, lane : lane + 1] * parts_ref[y, half * HD : (half + 1) * HD].astype(F32)
        rows_ref[half * HD : (half + 1) * HD] = acc / total
    x = jnp.concatenate([rows_ref[pl.ds(h, HD, stride=2), :].astype(BF) for h in range(2)], axis=1)
    for k, w_ref in enumerate((w0_ref, w1_ref)):
        w = jnp.concatenate([w_ref[z] for z in range(NZ)], axis=1)
        y = dot(x, w, 1, 0).astype(BF)
        for b in range(16):
            out_ref[b * 2 + k] = y[b * 8 : b * 8 + 8]


def sum_kernel(parts_ref, res_ref, out_ref):
    total = parts_ref[0].astype(F32)
    for i in range(1, 32):
        total = total + parts_ref[i].astype(F32)
    res = jnp.concatenate([res_ref[z] for z in range(NZ)], axis=1).astype(F32)
    block = (res + total).astype(BF)
    for i in range(32):
        out_ref[i] = block


def mlp_kernel(r_ref, w0_ref, w1_ref, out_ref):
    z = dot(r_ref[:, 0].reshape(HD, 4 * HD), w0_ref[...], 1, 0)
    z = z + dot(r_ref[:, 1].reshape(HD, 4 * HD), w1_ref[...], 1, 0)
    out_ref[...] = z.astype(BF)


def swap(x):
    return lax.ppermute(x, "c", [(0, 1), (1, 0)])


def exchange(x, axes):
    return lax.all_to_all(x, axes, 0, 0, tiled=True)


def on_device(queries, new_kv, own_kv, man_kv, pages, own_len, resid, w_out, w_gate, w_up):
    shape = jax.ShapeDtypeStruct
    core, zl, zh, x = (lax.axis_index(a) for a in ("c", "zl", "zh", "x"))
    half = w_gate.shape[1] // 2

    q_out = call(query_kernel, "queries", shape((CHIPS, 8, HD), BF), queries, scratch=[pltpu.VMEM((QROWS, HD), F32)])
    q_all = exchange(q_out, PLANE)
    kv = exchange(jnp.broadcast_to(man_kv.reshape(1, 2, 2 * PAGE, HD), (NZ, 2, 2 * PAGE, HD)), "zl")
    kv = lax.all_gather(kv, "c", axis=0, tiled=True)

    own = call(
        own_kernel, "own_attention", shape((CHIPS, 16, HD), BF),
        pages, own_len, q_out, new_kv, own_kv.reshape(2, POOL * PAGE, HD),
        specs=[SMEM, SMEM, VMEM, VMEM, VMEM],
    )
    own_all = exchange(own, PLANE)

    w_a = exchange(w_out.reshape(NZ, 2 * HD, HD), "zl")
    w_b = swap(w_a)
    cut = jnp.stack([w_gate[:, :half], w_gate[:, half:], w_up[:, :half], w_up[:, half:]])
    v_a = exchange(cut, "zl")
    v_b = swap(v_a)

    res = resid.reshape(NZ, 4, 2, 2, ROWS, HD)
    res = lax.dynamic_index_in_dim(res, zh * 2 + x // 2, 1, keepdims=False)
    res = exchange(res.transpose(0, 2, 1, 3, 4).reshape(2 * NZ, 8, HD), ("zl", "c"))
    res = lax.dynamic_index_in_dim(res.reshape(NZ, 2, 8, HD), (core + x) % 2, 1, keepdims=False)

    parts = exchange(call(man_kernel, "manifest_attention", shape((NY, 2 * HD + 8, HD), BF), q_all, kv), "y")
    projected = call(
        join_kernel, "join_project", shape((32, 8, 4 * HD), BF), parts, own_all, w_a, w_b,
        scratch=[pltpu.VMEM((2 * HD, HD), F32)],
    )
    summed = call(sum_kernel, "head_sum", shape((32, 8, 4 * HD), BF), exchange(projected, SIDE), res)
    rows = exchange(summed, SIDE).reshape(16, 2, 8, 4 * HD)
    z = call(
        mlp_kernel, "gate_up", shape((CHIPS * ROWS, half), BF),
        rows, v_a.reshape(4 * HD, half), v_b.reshape(4 * HD, half),
    )
    joined = exchange(z.reshape(CHIPS, ROWS, half), PLANE).reshape(NY, NZ, ROWS, half)
    joined = joined.astype(F32).sum(0)
    gate = jnp.concatenate([joined[0], joined[1]], axis=1)
    up = jnp.concatenate([joined[2], joined[3]], axis=1)
    hidden = (jax.nn.silu(gate) * up).astype(BF)

    chip = lax.dynamic_slice_in_dim(rows, zl * HD, HD, 3)
    kept = chip[:, 0].reshape(CHIPS, 1, ROWS, HD)
    given = swap(chip[:, 1]).reshape(CHIPS, 1, ROWS, HD)
    first = jnp.where(core == 0, kept, given)
    second = jnp.where(core == 0, given, kept)
    resid_out = jnp.concatenate([first, second], axis=1).reshape(CHIPS * 2 * ROWS, HD)
    return (resid_out, hidden)


def solution(mesh):
    fine = Mesh(mesh.devices.reshape(8, 4, 2, 2, 4), ("y", "zl", "c", "zh", "x"))
    in_specs = (
        P(REQ, HEAD),
        P(None, REQ, HEAD),
        P(None, REQ, None, HEAD),
        P(None, REQ, None, HEAD),
        P(REQ, None),
        P(REQ),
        P(None, REQ),
        P(HEAD, REQ),
        P(REQ, HEAD),
        P(REQ, HEAD),
    )
    out_specs = (P(None, REQ), P(REQ, HEAD))
    return jax.shard_map(
        on_device, mesh=fine, in_specs=in_specs, out_specs=out_specs, check_vma=False
    )
```

```python
import jax
import jax.numpy as jnp
from jax import lax
from jax.experimental import pallas as pl
from jax.experimental.pallas import tpu as pltpu
from jax.sharding import Mesh, PartitionSpec as P

HD = 128
PAGE = 64
MAXP = 8
GROUP = 8
ROWS = 4
QROWS = ROWS * GROUP
POOL = 32
NY = 8
NZ = 4
CHIPS = NY * NZ
SCALE = HD**-0.5
PLANE = ("y", "zl")
SIDE = ("zl", "zh", "x")
HEAD = ("zh", "x")
REQ = ("y", "zl", "c")
BF = jnp.bfloat16
F32 = jnp.float32
VMEM = pl.BlockSpec(memory_space=pltpu.VMEM)
SMEM = pl.BlockSpec(memory_space=pltpu.SMEM)


def dot(a, b, ca, cb):
    return lax.dot_general(a, b, (((ca,), (cb,)), ((), ())), preferred_element_type=F32)


def call(kernel, name, out_shape, *args, specs=None, scratch=()):
    return pl.pallas_call(
        kernel,
        out_shape=out_shape,
        in_specs=specs or [VMEM] * len(args),
        out_specs=jax.tree.map(lambda _: VMEM, out_shape),
        scratch_shapes=scratch,
        compiler_params=pltpu.CompilerParams(vmem_limit_bytes=40 << 20),
        name=name,
    )(*args)


def query_kernel(q_ref, out_ref, rows_ref):
    for h in range(GROUP):
        first = (h // 2) * 8 + h % 2
        rows_ref[pl.ds(first, ROWS, stride=2), :] = q_ref[:, h * HD : (h + 1) * HD].astype(F32)
    for z in range(NZ):
        block = rows_ref[z * 8 : z * 8 + 8].astype(BF)
        for y in range(NY):
            out_ref[y * NZ + z] = block


def own_kernel(zl_ref, pages_ref, len_ref, q_ref, new_ref, own_ref, man_ref, *refs):
    outs, (acc_ref, stats_ref) = refs[:NZ], refs[NZ:]
    tokens = POOL * PAGE
    q = q_ref[0:NZ].reshape(QROWS, HD)
    scores = dot(q, own_ref[0], 1, 1) * SCALE
    page_of = lax.broadcasted_iota(jnp.int32, (8, tokens), 1) // PAGE
    req = lax.broadcasted_iota(jnp.int32, (8, HD), 0) // 2

    def by_request(values):
        return jnp.where(req == 0, values[0], jnp.where(req == 1, values[1], jnp.where(req == 2, values[2], values[3])))

    count = jnp.zeros((8, tokens), F32)
    for i in range(MAXP):
        page = by_request([jnp.where(i < len_ref[b], pages_ref[b, i], -1) for b in range(ROWS)])
        count = count + jnp.where(page_of == page[:, 0:1], 1.0, 0.0)
    new_k = by_request([new_ref[0, b : b + 1].astype(F32) for b in range(ROWS)])
    new_v = by_request([new_ref[1, b : b + 1].astype(F32) for b in range(ROWS)])
    lane = lax.broadcasted_iota(jnp.int32, (8, HD), 1) % 32
    weights, news = [], []
    for z in range(NZ):
        s = jnp.where(count > 0.0, scores[z * 8 : z * 8 + 8], -jnp.inf)
        s_new = jnp.sum(q_ref[z].astype(F32) * new_k, axis=1, keepdims=True) * SCALE
        top = jnp.maximum(jnp.max(s, axis=1, keepdims=True), s_new).astype(BF).astype(F32)
        w = jnp.exp(s - top) * count
        w_new = jnp.exp(s_new - top)
        total = jnp.sum(w, axis=1, keepdims=True) + w_new
        high = total.astype(BF).astype(F32)
        weights.append(w.astype(BF))
        news.append(w_new.astype(BF).astype(F32) * new_v)
        stats_ref[z * 8 : z * 8 + 8] = jnp.where(
            lane == 0, top, jnp.where(lane == 1, high, jnp.where(lane == 2, total - high, 0.0))
        )
    acc = dot(jnp.concatenate(weights, axis=0), own_ref[1], 1, 0)
    acc_ref[...] = acc + jnp.concatenate(news, axis=0)
    for s in range(NZ):
        to = pl.ds(pl.multiple_of((zl_ref[0] + s) % NZ * 8, 8), 8)
        outs[s][0 : 4 * PAGE] = man_ref[...]
        outs[s][4 * PAGE :] = jnp.concatenate([acc_ref[to, :], stats_ref[to, :]], axis=0).astype(BF)


def man_kernel(zl_ref, q_ref, kv_ref, p0_ref, p1_ref, p2_ref, p3_ref, out_ref, own_ref):
    n = 2 * NZ
    keys = jnp.concatenate([kv_ref[i, 0] for i in range(n)], axis=0)
    values = jnp.concatenate([kv_ref[i, 1] for i in range(n)], axis=0)
    row = lax.broadcasted_iota(jnp.int32, (8, HD), 0)
    lane = lax.broadcasted_iota(jnp.int32, (8, HD), 1) // 32
    stats = jnp.zeros((8, HD), F32)
    own_stats = jnp.zeros((8, HD), F32)
    for s, p_ref in enumerate((p0_ref, p1_ref, p2_ref, p3_ref)):
        source = (zl_ref[0] + NZ - s) % NZ
        block = p_ref[4 * PAGE :].astype(F32)
        own_ref[pl.ds(pl.multiple_of(source * 8, 8), 8), :] = block[0:8]
        own_stats = jnp.where(lane == source, block[8:16], own_stats)
    accs = []
    for half in range(2):
        q = q_ref[half * 16 : half * 16 + 16].reshape(HD, HD)
        s = dot(keys, q, 1, 1) * SCALE
        top = jnp.max(s, axis=0, keepdims=True).astype(BF).astype(F32)
        w = jnp.exp(s - top)
        total = jnp.sum(w, axis=0, keepdims=True)
        high = total.astype(BF).astype(F32)
        accs.append(dot(w.astype(BF), values, 0, 0))
        for k, value in enumerate((top, high, total - high)):
            stats = jnp.where(row == 3 * half + k, value, stats)
    block = jnp.concatenate(accs + [stats, own_ref[...], own_stats], axis=0).astype(BF)
    for y in range(NY):
        out_ref[y] = block


def join_kernel(zl_ref, parts_ref, w0_ref, w1_ref, out_ref, rows_ref):
    rows = 2 * HD
    stats = parts_ref[:, rows : rows + 8, :].reshape(NY * 8, HD)
    eye = lax.broadcasted_iota(jnp.int32, (HD, HD), 0) == lax.broadcasted_iota(jnp.int32, (HD, HD), 1)
    s = dot(jnp.where(eye, 1.0, 0.0).astype(BF), stats, 1, 1)
    n = NY * 8
    kind = lax.broadcasted_iota(jnp.int32, (HD, n), 1) % 8
    for half in range(2):
        base = 3 * half
        own_acc, own_stats = [], []
        for y in range(half * 4, half * 4 + 4):
            own = parts_ref[y, rows + 8 : rows + 48].astype(F32)
            own_acc.append(own[0:32])
            own_stats += [own[32:40, z * 32 : z * 32 + 3] for z in range(NZ)]
        own_acc = jnp.concatenate(own_acc, axis=0)
        own_stats = jnp.concatenate(own_stats, axis=0)
        own_top = own_stats[:, 0:1]
        here = kind == base
        top = jnp.maximum(jnp.max(jnp.where(here, s, -jnp.inf), axis=1, keepdims=True), own_top)
        factor = jnp.where(here, jnp.exp(jnp.minimum(s - top, 0.0)), 0.0)
        totals = jnp.concatenate([s[:, 1:], s[:, :1]], axis=1) + jnp.concatenate([s[:, 2:], s[:, :2]], axis=1)
        own_factor = jnp.exp(own_top - top)
        total = jnp.sum(factor * totals, axis=1, keepdims=True) + own_factor * (own_stats[:, 1:2] + own_stats[:, 2:3])
        acc = own_factor * own_acc
        for y in range(NY):
            lane = y * 8 + base
            acc = acc + factor[:, lane : lane + 1] * parts_ref[y, half * HD : (half + 1) * HD].astype(F32)
        rows_ref[half * HD : (half + 1) * HD] = acc / total
    x = jnp.concatenate([rows_ref[pl.ds(h, HD, stride=2), :].astype(BF) for h in range(2)], axis=1)
    for k, w_ref in enumerate((w0_ref, w1_ref)):
        w = jnp.concatenate([w_ref[(zl_ref[0] + NZ - z) % NZ, 0 : 2 * HD] for z in range(NZ)], axis=1)
        y = dot(x, w, 1, 0).astype(BF)
        for b in range(16):
            out_ref[b * 2 + k] = y[b * 8 : b * 8 + 8]


def sum_kernel(place_ref, parts_ref, res0_ref, res1_ref, out_ref):
    total = parts_ref[0].astype(F32)
    for i in range(1, 32):
        total = total + parts_ref[i].astype(F32)
    at = [(place_ref[0] + NZ - z) % NZ for z in range(NZ)]
    res0 = jnp.concatenate([res0_ref[i, 2 * HD :] for i in at], axis=1).astype(F32)
    res1 = jnp.concatenate([res1_ref[i, 2 * HD :] for i in at], axis=1).astype(F32)
    block = (jnp.where(place_ref[1] == 0, res0, res1) + total).astype(BF)
    for i in range(32):
        out_ref[i] = block


def mlp_kernel(zl_ref, r_ref, w0_ref, w1_ref, out_ref):
    at = [(zl_ref[0] + NZ - z) % NZ for z in range(NZ)]
    z = dot(r_ref[:, 0].reshape(HD, 4 * HD), jnp.concatenate([w0_ref[i] for i in at], axis=0), 1, 0)
    z = z + dot(r_ref[:, 1].reshape(HD, 4 * HD), jnp.concatenate([w1_ref[i] for i in at], axis=0), 1, 0)
    out_ref[...] = z.astype(BF)


def shifted(pieces):
    return [pieces[0]] + [
        lax.ppermute(pieces[s], "zl", [(i, (i + s) % NZ) for i in range(NZ)]) for s in range(1, NZ)
    ]


def swap(x):
    return lax.ppermute(x, "c", [(0, 1), (1, 0)])


def exchange(x, axes):
    return lax.all_to_all(x, axes, 0, 0, tiled=True)


def on_device(queries, new_kv, own_kv, man_kv, pages, own_len, resid, w_out, w_gate, w_up):
    shape = jax.ShapeDtypeStruct
    core, zl, zh, x = (lax.axis_index(a) for a in ("c", "zl", "zh", "x"))
    half = w_gate.shape[1] // 2
    place = jnp.stack([zl, x % 2]).astype(jnp.int32)

    q_out = call(query_kernel, "queries", shape((CHIPS, 8, HD), BF), queries, scratch=[pltpu.VMEM((QROWS, HD), F32)])
    q_all = exchange(q_out, PLANE)
    pieces = call(
        own_kernel, "own_attention", [shape((4 * PAGE + 16, HD), BF)] * NZ,
        place, pages, own_len, q_out, new_kv, own_kv.reshape(2, POOL * PAGE, HD), man_kv.reshape(4 * PAGE, HD),
        specs=[SMEM, SMEM, SMEM, VMEM, VMEM, VMEM, VMEM], scratch=[pltpu.VMEM((QROWS, HD), F32)] * 2,
    )
    pieces = shifted(pieces)
    kv = jnp.stack([p[: 4 * PAGE].reshape(2, 2 * PAGE, HD) for p in pieces])
    kv = lax.all_gather(kv, "c", axis=0, tiled=True)

    res = resid.reshape(NZ, 4, 2, 2, ROWS, HD)
    res = lax.dynamic_index_in_dim(res, zh * 2 + x // 2, 1, keepdims=False)
    res = lax.dynamic_index_in_dim(res, (core + x) % 2, 2, keepdims=False).reshape(NZ, 8, HD)
    w_cut = jnp.concatenate([w_out.reshape(NZ, 2 * HD, HD), res], axis=1)
    w_cut, q_all = lax.optimization_barrier((w_cut, q_all))
    at = [(zl + s) % NZ for s in range(NZ)]
    w_a = jnp.stack(shifted([lax.dynamic_index_in_dim(w_cut, i, 0, keepdims=False) for i in at]))
    w_b = swap(w_a)
    (w_gate, w_up), kv = lax.optimization_barrier(((w_gate, w_up), kv))
    v_cut = jnp.stack([w_gate[:, :half], w_gate[:, half:], w_up[:, :half], w_up[:, half:]])
    v_a = jnp.stack(shifted([lax.dynamic_index_in_dim(v_cut, i, 0, keepdims=False) for i in at]))
    v_b = swap(v_a)

    man = call(
        man_kernel, "manifest_attention", shape((NY, 2 * HD + 48, HD), BF), place, q_all, kv, *pieces,
        specs=[SMEM] + [VMEM] * 6, scratch=[pltpu.VMEM((QROWS, HD), F32)],
    )
    projected = call(
        join_kernel, "join_project", shape((32, 8, 4 * HD), BF), place, exchange(man, "y"), w_a, w_b,
        specs=[SMEM] + [VMEM] * 3, scratch=[pltpu.VMEM((2 * HD, HD), F32)],
    )
    summed = call(
        sum_kernel, "head_sum", shape((32, 8, 4 * HD), BF), place, exchange(projected, SIDE), w_a, w_b,
        specs=[SMEM] + [VMEM] * 3,
    )
    rows = exchange(summed, SIDE).reshape(16, 2, 8, 4 * HD)
    z = call(
        mlp_kernel, "gate_up", shape((CHIPS * ROWS, half), BF), place, rows, v_a, v_b, specs=[SMEM] + [VMEM] * 3
    )
    joined = exchange(z.reshape(CHIPS, ROWS, half), PLANE).reshape(NY, NZ, ROWS, half)
    joined = joined.astype(F32).sum(0)
    gate = jnp.concatenate([joined[0], joined[1]], axis=1)
    up = jnp.concatenate([joined[2], joined[3]], axis=1)
    hidden = (jax.nn.silu(gate) * up).astype(BF)

    chip = lax.dynamic_slice_in_dim(rows, zl * HD, HD, 3)
    kept = chip[:, 0].reshape(CHIPS, 1, ROWS, HD)
    given = swap(chip[:, 1]).reshape(CHIPS, 1, ROWS, HD)
    first = jnp.where(core == 0, kept, given)
    second = jnp.where(core == 0, given, kept)
    resid_out = jnp.concatenate([first, second], axis=1).reshape(CHIPS * 2 * ROWS, HD)
    return (resid_out, hidden)


def solution(mesh):
    fine = Mesh(mesh.devices.reshape(8, 4, 2, 2, 4), ("y", "zl", "c", "zh", "x"))
    in_specs = (
        P(REQ, HEAD),
        P(None, REQ, HEAD),
        P(None, REQ, None, HEAD),
        P(None, REQ, None, HEAD),
        P(REQ, None),
        P(REQ),
        P(None, REQ),
        P(HEAD, REQ),
        P(REQ, HEAD),
        P(REQ, HEAD),
    )
    out_specs = (P(None, REQ), P(REQ, HEAD))
    return jax.shard_map(
        on_device, mesh=fine, in_specs=in_specs, out_specs=out_specs, check_vma=False
    )
```

```python
import jax
import jax.numpy as jnp
from jax import lax
from jax.experimental import pallas as pl
from jax.experimental.pallas import tpu as pltpu
from jax.sharding import Mesh, PartitionSpec as P

HD = 128
PAGE = 64
MAXP = 8
GROUP = 8
ROWS = 4
QROWS = ROWS * GROUP
POOL = 32
CHIPS = 32
PEERS = 16
STATS = 8
SCALE = HD**-0.5
PLANE = ("y", "zq", "p")
SPARSE = ("y", "zq")
HEAD = ("zh", "x")
REQ = ("y", "zq", "p", "c")
BF = jnp.bfloat16
F32 = jnp.float32


def dot(a, b, ca, cb):
    return lax.dot_general(a, b, (((ca,), (cb,)), ((), ())), preferred_element_type=F32)


def own_kernel(pages_ref, len_ref, q_ref, new_ref, own_ref, acc_ref, top_ref, total_ref):
    tokens = POOL * PAGE
    scores = dot(q_ref[...], own_ref[0], 1, 1) * SCALE
    page_of = lax.broadcasted_iota(jnp.int32, (GROUP, tokens), 1) // PAGE
    weights, tops, totals, news = [], [], [], []
    for b in range(ROWS):
        count = jnp.zeros((GROUP, tokens), F32)
        for i in range(MAXP):
            page = jnp.where(i < len_ref[b], pages_ref[b, i], -1)
            count = count + jnp.where(page_of == page, 1.0, 0.0)
        s = jnp.where(count > 0.0, scores[b * GROUP : (b + 1) * GROUP], -jnp.inf)
        q = q_ref[b * GROUP : (b + 1) * GROUP].astype(F32)
        s_new = jnp.sum(q * new_ref[0, b : b + 1].astype(F32), axis=1, keepdims=True) * SCALE
        top = jnp.maximum(jnp.max(s, axis=1, keepdims=True), s_new)
        w = jnp.exp(s - top) * count
        w_new = jnp.exp(s_new - top)
        weights.append(w.astype(BF))
        tops.append(top)
        totals.append(jnp.sum(w, axis=1, keepdims=True) + w_new)
        news.append(w_new.astype(BF).astype(F32) * new_ref[1, b : b + 1].astype(F32))
    acc = dot(jnp.concatenate(weights, axis=0), own_ref[1], 1, 0)
    acc_ref[...] = acc + jnp.concatenate(news, axis=0)
    top_ref[...] = jnp.broadcast_to(jnp.concatenate(tops, axis=0), (QROWS, HD))
    total_ref[...] = jnp.broadcast_to(jnp.concatenate(totals, axis=0), (QROWS, HD))


def own_part(pages, own_len, q, new_kv, own_kv):
    smem = pl.BlockSpec(memory_space=pltpu.SMEM)
    vmem = pl.BlockSpec(memory_space=pltpu.VMEM)
    return pl.pallas_call(
        own_kernel,
        out_shape=[jax.ShapeDtypeStruct((QROWS, HD), F32)] * 3,
        in_specs=[smem, smem, vmem, vmem, vmem],
        out_specs=[vmem] * 3,
        compiler_params=pltpu.CompilerParams(vmem_limit_bytes=32 << 20),
        name="own_attention",
    )(pages, own_len, q, new_kv, own_kv)


def man_kernel(q_ref, kv_ref, out_ref):
    keys = jnp.concatenate([kv_ref[i, 0] for i in range(4)], axis=0)
    values = jnp.concatenate([kv_ref[i, 1] for i in range(4)], axis=0)
    row = lax.broadcasted_iota(jnp.int32, (STATS, HD), 0)
    for chunk in range(PEERS * QROWS // HD):
        s = dot(keys, q_ref[chunk * HD : (chunk + 1) * HD], 1, 1) * SCALE
        top = jnp.max(s, axis=0, keepdims=True).astype(BF).astype(F32)
        w = jnp.exp(s - top)
        total = jnp.sum(w, axis=0, keepdims=True)
        high = total.astype(BF).astype(F32)
        acc = dot(w.astype(BF), values, 0, 0).astype(BF)
        stats = jnp.where(row == 0, top, jnp.where(row == 1, high, jnp.where(row == 2, total - high, 0.0)))
        stats = stats.astype(BF)
        for j in range(HD // QROWS):
            to = chunk * (HD // QROWS) + j
            out_ref[to, 0:QROWS] = acc[j * QROWS : (j + 1) * QROWS]
            out_ref[to, QROWS : QROWS + STATS] = stats


def man_part(q_all, kv):
    vmem = pl.BlockSpec(memory_space=pltpu.VMEM)
    return pl.pallas_call(
        man_kernel,
        out_shape=jax.ShapeDtypeStruct((PEERS, QROWS + STATS, HD), BF),
        in_specs=[vmem, vmem],
        out_specs=vmem,
        compiler_params=pltpu.CompilerParams(vmem_limit_bytes=32 << 20),
        name="manifest_attention",
    )(q_all, kv)


def join_kernel(place_ref, parts_ref, acc_ref, top_ref, total_ref, out_ref, rows_ref):
    stats = parts_ref[:, QROWS : QROWS + STATS, :].reshape(PEERS * STATS, HD)
    lane = lax.broadcasted_iota(jnp.int32, (QROWS, HD), 1)
    row = lax.broadcasted_iota(jnp.int32, (QROWS, HD), 0)
    pick = jnp.where(lane == row + place_ref[0] * QROWS, 1.0, 0.0).astype(BF)
    s = dot(pick, stats, 1, 1)
    n = PEERS * STATS
    kind = lax.broadcasted_iota(jnp.int32, (QROWS, n), 1) % STATS
    totals = pltpu.roll(s, n - 1, 1) + pltpu.roll(s, n - 2, 1)
    own_top = top_ref[:, 0:1]
    top = jnp.maximum(jnp.max(jnp.where(kind == 0, s, -jnp.inf), axis=1, keepdims=True), own_top)
    factor = jnp.where(kind == 0, jnp.exp(jnp.minimum(s - top, 0.0)), 0.0)
    own_factor = jnp.exp(own_top - top)
    total = jnp.sum(factor * totals, axis=1, keepdims=True) + own_factor * total_ref[:, 0:1]
    acc = own_factor * acc_ref[...]
    for i in range(PEERS):
        acc = acc + factor[:, i * STATS : i * STATS + 1] * parts_ref[i, 0:QROWS].astype(F32)
    rows_ref[...] = acc / total
    for h in range(GROUP):
        rows = rows_ref[pl.ds(h, ROWS, stride=GROUP), :].astype(BF)
        for i in range(CHIPS):
            out_ref[i, :, h * HD : (h + 1) * HD] = rows


def join_part(place, parts, acc, top, total):
    smem = pl.BlockSpec(memory_space=pltpu.SMEM)
    vmem = pl.BlockSpec(memory_space=pltpu.VMEM)
    return pl.pallas_call(
        join_kernel,
        out_shape=jax.ShapeDtypeStruct((CHIPS, ROWS, GROUP * HD), BF),
        in_specs=[smem, vmem, vmem, vmem, vmem],
        out_specs=vmem,
        scratch_shapes=[pltpu.VMEM((QROWS, HD), F32)],
        compiler_params=pltpu.CompilerParams(vmem_limit_bytes=32 << 20),
        name="join_attention",
    )(place, parts, acc, top, total)


def swap(x):
    return lax.ppermute(x, "c", [(0, 1), (1, 0)])


def pair(x):
    return lax.ppermute(x, "p", [(0, 1), (1, 0)])


def exchange(x, axes):
    return lax.all_to_all(x, axes, 0, 0, tiled=True)


def on_device(queries, new_kv, own_kv, man_kv, pages, own_len, resid, w_out, w_gate, w_up):
    core, side = lax.axis_index("c"), lax.axis_index("p")
    width = w_gate.shape[1]
    q = queries.reshape(QROWS, HD)
    kv = man_kv.reshape(2, 2 * PAGE, HD)
    kv = lax.all_gather(jnp.stack([kv, pair(kv)]), "c", axis=0, tiled=True)
    w_out2 = jnp.concatenate([w_out, swap(w_out)], axis=1)
    w_keep = jnp.where(side == 0, w_gate, w_up)
    w_pair = pair(jnp.where(side == 0, w_up, w_gate))
    w_keep2 = jnp.concatenate([w_keep, swap(w_keep)], axis=0)
    res = resid.reshape(CHIPS, 2, ROWS, HD)
    mine = jnp.where(core == 0, res[:, 0], res[:, 1])
    theirs = swap(jnp.where(core == 0, res[:, 1], res[:, 0]))
    res2 = jnp.concatenate([mine, theirs], axis=-1).reshape(CHIPS * ROWS, 2 * HD)

    acc, top, total = own_part(pages, own_len, q, new_kv, own_kv.reshape(2, POOL * PAGE, HD))
    q_all = exchange(jnp.broadcast_to(q[None], (PEERS, QROWS, HD)), SPARSE).reshape(PEERS * QROWS, HD)
    parts = exchange(man_part(q_all, kv), SPARSE)
    place = (lax.axis_index(SPARSE) % 4).astype(jnp.int32).reshape(1)
    attn = exchange(join_part(place, parts, acc, top, total), PLANE).reshape(CHIPS * ROWS, GROUP * HD)
    attn, w_pair = lax.optimization_barrier((attn, w_pair))
    w_pair2 = jnp.concatenate([w_pair, swap(w_pair)], axis=0)

    partial_out = jnp.dot(attn, w_out2, preferred_element_type=F32).astype(BF)
    heads = exchange(jnp.broadcast_to(partial_out[None], (8, *partial_out.shape)), HEAD)
    out2 = (res2.astype(F32) + heads.astype(F32).sum(0)).astype(BF)

    z = jnp.dot(out2, w_keep2, preferred_element_type=F32)
    z = (z + jnp.dot(pair(out2), w_pair2, preferred_element_type=F32)).astype(BF)
    joined = exchange(z.reshape(CHIPS, ROWS, width), PLANE).reshape(PEERS, 2, ROWS, width)
    joined = joined.astype(F32).sum(0)
    hidden = (jax.nn.silu(joined[0]) * joined[1]).astype(BF)

    kept = out2[:, :HD].reshape(CHIPS, 1, ROWS, HD)
    given = swap(out2[:, HD:]).reshape(CHIPS, 1, ROWS, HD)
    first = jnp.where(core == 0, kept, given)
    second = jnp.where(core == 0, given, kept)
    resid_out = jnp.concatenate([first, second], axis=1).reshape(CHIPS * 2 * ROWS, HD)
    return (resid_out, hidden)


def solution(mesh):
    fine = Mesh(mesh.devices.reshape(8, 2, 2, 2, 2, 4), ("y", "zq", "p", "c", "zh", "x"))
    in_specs = (
        P(REQ, HEAD),
        P(None, REQ, HEAD),
        P(None, REQ, None, HEAD),
        P(None, REQ, None, HEAD),
        P(REQ, None),
        P(REQ),
        P(None, REQ),
        P(HEAD, REQ),
        P(REQ, HEAD),
        P(REQ, HEAD),
    )
    out_specs = (P(None, REQ), P(REQ, HEAD))
    return jax.shard_map(
        on_device, mesh=fine, in_specs=in_specs, out_specs=out_specs, check_vma=False
    )
```

```python
import jax
import jax.numpy as jnp
from jax import lax
from jax.experimental import pallas as pl
from jax.experimental.pallas import tpu as pltpu
from jax.sharding import Mesh, PartitionSpec as P

HD = 128
PAGE = 64
MAXP = 8
GROUP = 8
ROWS = 4
QROWS = ROWS * GROUP
POOL = 32
PEERS = 16
STATS = 8
SCALE = HD**-0.5
SPARSE = ("y", "zq")
HEAD = ("zh", "x")
REQ = ("y", "zq", "p", "c")
BF = jnp.bfloat16
F32 = jnp.float32


def dot(a, b, ca, cb):
    return lax.dot_general(a, b, (((ca,), (cb,)), ((), ())), preferred_element_type=F32)


def own_kernel(pages_ref, len_ref, q_ref, new_ref, own_ref, acc_ref, top_ref, total_ref):
    tokens = POOL * PAGE
    scores = dot(q_ref[...], own_ref[0], 1, 1) * SCALE
    page_of = lax.broadcasted_iota(jnp.int32, (GROUP, tokens), 1) // PAGE
    weights, tops, totals, news = [], [], [], []
    for b in range(ROWS):
        count = jnp.zeros((GROUP, tokens), F32)
        for i in range(MAXP):
            page = jnp.where(i < len_ref[b], pages_ref[b, i], -1)
            count = count + jnp.where(page_of == page, 1.0, 0.0)
        s = jnp.where(count > 0.0, scores[b * GROUP : (b + 1) * GROUP], -jnp.inf)
        q = q_ref[b * GROUP : (b + 1) * GROUP].astype(F32)
        s_new = jnp.sum(q * new_ref[0, b : b + 1].astype(F32), axis=1, keepdims=True) * SCALE
        top = jnp.maximum(jnp.max(s, axis=1, keepdims=True), s_new)
        w = jnp.exp(s - top) * count
        w_new = jnp.exp(s_new - top)
        weights.append(w.astype(BF))
        tops.append(top)
        totals.append(jnp.sum(w, axis=1, keepdims=True) + w_new)
        news.append(w_new.astype(BF).astype(F32) * new_ref[1, b : b + 1].astype(F32))
    acc = dot(jnp.concatenate(weights, axis=0), own_ref[1], 1, 0)
    acc_ref[...] = acc + jnp.concatenate(news, axis=0)
    top_ref[...] = jnp.broadcast_to(jnp.concatenate(tops, axis=0), (QROWS, HD))
    total_ref[...] = jnp.broadcast_to(jnp.concatenate(totals, axis=0), (QROWS, HD))


def own_part(pages, own_len, q, new_kv, own_kv):
    smem = pl.BlockSpec(memory_space=pltpu.SMEM)
    vmem = pl.BlockSpec(memory_space=pltpu.VMEM)
    return pl.pallas_call(
        own_kernel,
        out_shape=[jax.ShapeDtypeStruct((QROWS, HD), F32)] * 3,
        in_specs=[smem, smem, vmem, vmem, vmem],
        out_specs=[vmem] * 3,
        compiler_params=pltpu.CompilerParams(vmem_limit_bytes=32 << 20),
        name="own_attention",
    )(pages, own_len, q, new_kv, own_kv)


def man_kernel(q_ref, kv_ref, out_ref):
    keys = jnp.concatenate([kv_ref[i, 0] for i in range(4)], axis=0)
    values = jnp.concatenate([kv_ref[i, 1] for i in range(4)], axis=0)
    row = lax.broadcasted_iota(jnp.int32, (STATS, HD), 0)
    for chunk in range(PEERS * QROWS // HD):
        s = dot(keys, q_ref[chunk * HD : (chunk + 1) * HD], 1, 1) * SCALE
        top = jnp.max(s, axis=0, keepdims=True).astype(BF).astype(F32)
        w = jnp.exp(s - top)
        total = jnp.sum(w, axis=0, keepdims=True)
        high = total.astype(BF).astype(F32)
        acc = dot(w.astype(BF), values, 0, 0).astype(BF)
        stats = jnp.where(row == 0, top, jnp.where(row == 1, high, jnp.where(row == 2, total - high, 0.0)))
        stats = stats.astype(BF)
        for j in range(HD // QROWS):
            to = chunk * (HD // QROWS) + j
            out_ref[to, 0:QROWS] = acc[j * QROWS : (j + 1) * QROWS]
            out_ref[to, QROWS : QROWS + STATS] = stats


def man_part(q_all, kv):
    vmem = pl.BlockSpec(memory_space=pltpu.VMEM)
    return pl.pallas_call(
        man_kernel,
        out_shape=jax.ShapeDtypeStruct((PEERS, QROWS + STATS, HD), BF),
        in_specs=[vmem, vmem],
        out_specs=vmem,
        compiler_params=pltpu.CompilerParams(vmem_limit_bytes=32 << 20),
        name="manifest_attention",
    )(q_all, kv)


def join_kernel(place_ref, parts_ref, acc_ref, top_ref, total_ref, out_ref, rows_ref):
    stats = parts_ref[:, QROWS : QROWS + STATS, :].reshape(PEERS * STATS, HD)
    lane = lax.broadcasted_iota(jnp.int32, (QROWS, HD), 1)
    row = lax.broadcasted_iota(jnp.int32, (QROWS, HD), 0)
    pick = jnp.where(lane == row + place_ref[0] * QROWS, 1.0, 0.0).astype(BF)
    s = dot(pick, stats, 1, 1)
    n = PEERS * STATS
    kind = lax.broadcasted_iota(jnp.int32, (QROWS, n), 1) % STATS
    totals = pltpu.roll(s, n - 1, 1) + pltpu.roll(s, n - 2, 1)
    own_top = top_ref[:, 0:1]
    top = jnp.maximum(jnp.max(jnp.where(kind == 0, s, -jnp.inf), axis=1, keepdims=True), own_top)
    factor = jnp.where(kind == 0, jnp.exp(jnp.minimum(s - top, 0.0)), 0.0)
    own_factor = jnp.exp(own_top - top)
    total = jnp.sum(factor * totals, axis=1, keepdims=True) + own_factor * total_ref[:, 0:1]
    acc = own_factor * acc_ref[...]
    for i in range(PEERS):
        acc = acc + factor[:, i * STATS : i * STATS + 1] * parts_ref[i, 0:QROWS].astype(F32)
    rows_ref[...] = acc / total
    for h in range(GROUP):
        rows = rows_ref[pl.ds(h, ROWS, stride=GROUP), :].astype(BF)
        for i in range(PEERS):
            out_ref[i, :, h * HD : (h + 1) * HD] = rows


def join_part(place, parts, acc, top, total):
    smem = pl.BlockSpec(memory_space=pltpu.SMEM)
    vmem = pl.BlockSpec(memory_space=pltpu.VMEM)
    return pl.pallas_call(
        join_kernel,
        out_shape=jax.ShapeDtypeStruct((PEERS, ROWS, GROUP * HD), BF),
        in_specs=[smem, vmem, vmem, vmem, vmem],
        out_specs=vmem,
        scratch_shapes=[pltpu.VMEM((QROWS, HD), F32)],
        compiler_params=pltpu.CompilerParams(vmem_limit_bytes=32 << 20),
        name="join_attention",
    )(place, parts, acc, top, total)


def project_kernel(x_ref, w0_ref, w1_ref, w2_ref, w3_ref, out_ref):
    for k, w_ref in enumerate((w0_ref, w1_ref, w2_ref, w3_ref)):
        y = dot(x_ref[...], w_ref[...], 1, 0).astype(BF)
        for i in range(8):
            out_ref[i, :, k * HD : (k + 1) * HD] = y


def mlp_kernel(x_ref, g0_ref, g1_ref, g2_ref, g3_ref, u0_ref, u1_ref, u2_ref, u3_ref, out_ref):
    def product(*w_refs):
        w = [w_ref[...] for w_ref in w_refs]
        low = dot(x_ref[:, 0 : 2 * HD], jnp.concatenate(w[:2], axis=0), 1, 0)
        return low + dot(x_ref[:, 2 * HD :], jnp.concatenate(w[2:], axis=0), 1, 0)

    gate = product(g0_ref, g1_ref, g2_ref, g3_ref)
    up = product(u0_ref, u1_ref, u2_ref, u3_ref)
    for j in range(PEERS):
        at = slice(j * ROWS, (j + 1) * ROWS)
        out_ref[j] = jnp.concatenate([gate[at], up[at]], axis=0).astype(BF)


def dense(kernel, name, out_shape, *args):
    vmem = pl.BlockSpec(memory_space=pltpu.VMEM)
    return pl.pallas_call(
        kernel,
        out_shape=jax.ShapeDtypeStruct(out_shape, BF),
        in_specs=[vmem] * len(args),
        out_specs=vmem,
        compiler_params=pltpu.CompilerParams(vmem_limit_bytes=40 << 20),
        name=name,
    )(*args)


def swap(x):
    return lax.ppermute(x, "c", [(0, 1), (1, 0)])


def pair(x):
    return lax.ppermute(x, "p", [(0, 1), (1, 0)])


def exchange(x, axes):
    return lax.all_to_all(x, axes, 0, 0, tiled=True)


def pick(x, index, axis):
    return jnp.where(index == 0, lax.index_in_dim(x, 0, axis, False), lax.index_in_dim(x, 1, axis, False))


def ordered(own, other, index, axis):
    return jnp.where(index == 0, jnp.stack([own, other], axis), jnp.stack([other, own], axis))


def on_device(queries, new_kv, own_kv, man_kv, pages, own_len, resid, w_out, w_gate, w_up):
    core, side = lax.axis_index("c"), lax.axis_index("p")
    tie = lax.optimization_barrier
    width = w_gate.shape[1]
    rows = PEERS * ROWS
    q = queries.reshape(QROWS, HD)
    q_all = exchange(jnp.broadcast_to(q[None], (PEERS, QROWS, HD)), SPARSE).reshape(PEERS * QROWS, HD)
    kv = man_kv.reshape(2, 2 * PAGE, HD)
    kv = lax.all_gather(jnp.stack([kv, pair(kv)]), "c", axis=0, tiled=True)
    own = own_part(pages, own_len, q, new_kv, own_kv.reshape(2, POOL * PAGE, HD))
    q_all, kv, own = tie((q_all, kv, own))
    parts = exchange(man_part(q_all, kv), SPARSE)
    w_out_p = pair(w_out)
    parts, w_out_p, w_out_c, w_out_pc = tie((parts, w_out_p, swap(w_out), swap(w_out_p)))
    place = (lax.axis_index(SPARSE) % 4).astype(jnp.int32).reshape(1)
    attn = exchange(join_part(place, parts, *own), SPARSE).reshape(rows, GROUP * HD)
    res = resid.reshape(PEERS, 2, 2, ROWS, HD)
    res = jnp.stack([pick(res, core, 2), swap(pick(res, 1 - core, 2))], axis=3)
    attn, w_gate_p, w_up_p, res = tie((attn, pair(w_gate), pair(w_up), res))
    res = jnp.stack([pick(res, side, 1), pair(pick(res, 1 - side, 1))], axis=2).reshape(rows, 4 * HD)

    heads = exchange(dense(project_kernel, "project", (8, rows, 4 * HD), attn, w_out, w_out_c, w_out_p, w_out_pc), HEAD)
    out4 = (res.astype(F32) + heads.astype(F32).sum(0)).astype(BF)
    both = dense(
        mlp_kernel, "gate_up", (PEERS, 2 * ROWS, width), out4,
        w_gate, swap(w_gate), w_gate_p, swap(w_gate_p), w_up, swap(w_up), w_up_p, swap(w_up_p),
    )
    joined = exchange(both, SPARSE).astype(F32).sum(0)
    hidden = (jax.nn.silu(joined[:ROWS]) * joined[ROWS:]).astype(BF)

    out = out4.reshape(PEERS, ROWS, 2, 2, HD)
    out = ordered(out[:, :, 0], pair(out[:, :, 1]), side, 1)
    out = ordered(out[:, :, :, 0], swap(out[:, :, :, 1]), core, 2)
    return (out.reshape(PEERS * 4 * ROWS, HD), hidden)


def solution(mesh):
    fine = Mesh(mesh.devices.reshape(8, 2, 2, 2, 2, 4), ("y", "zq", "p", "c", "zh", "x"))
    in_specs = (
        P(REQ, HEAD),
        P(None, REQ, HEAD),
        P(None, REQ, None, HEAD),
        P(None, REQ, None, HEAD),
        P(REQ, None),
        P(REQ),
        P(None, REQ),
        P(HEAD, REQ),
        P(REQ, HEAD),
        P(REQ, HEAD),
    )
    out_specs = (P(None, REQ), P(REQ, HEAD))
    return jax.shard_map(
        on_device, mesh=fine, in_specs=in_specs, out_specs=out_specs, check_vma=False
    )
```

```python
import jax
import jax.numpy as jnp
from jax import lax
from jax.experimental import pallas as pl
from jax.experimental.pallas import tpu as pltpu
from jax.sharding import Mesh, PartitionSpec as P

HD = 128
PAGE = 64
MAXP = 8
GROUP = 8
ROWS = 4
QROWS = ROWS * GROUP
POOL = 32
CHIPS = 32
PEERS = 16
STATS = 8
SCALE = HD**-0.5
PLANE = ("y", "zq", "p")
SPARSE = ("y", "zq")
HEAD = ("zh", "x")
REQ = ("y", "zq", "p", "c")
BF = jnp.bfloat16
F32 = jnp.float32


def dot(a, b, ca, cb):
    return lax.dot_general(a, b, (((ca,), (cb,)), ((), ())), preferred_element_type=F32)


def own_kernel(pages_ref, len_ref, q_ref, new_ref, own_ref, acc_ref, top_ref, total_ref):
    tokens = POOL * PAGE
    scores = dot(q_ref[...], own_ref[0], 1, 1) * SCALE
    page_of = lax.broadcasted_iota(jnp.int32, (GROUP, tokens), 1) // PAGE
    weights, tops, totals, news = [], [], [], []
    for b in range(ROWS):
        count = jnp.zeros((GROUP, tokens), F32)
        for i in range(MAXP):
            page = jnp.where(i < len_ref[b], pages_ref[b, i], -1)
            count = count + jnp.where(page_of == page, 1.0, 0.0)
        s = jnp.where(count > 0.0, scores[b * GROUP : (b + 1) * GROUP], -jnp.inf)
        q = q_ref[b * GROUP : (b + 1) * GROUP].astype(F32)
        s_new = jnp.sum(q * new_ref[0, b : b + 1].astype(F32), axis=1, keepdims=True) * SCALE
        top = jnp.maximum(jnp.max(s, axis=1, keepdims=True), s_new)
        w = jnp.exp(s - top) * count
        w_new = jnp.exp(s_new - top)
        weights.append(w.astype(BF))
        tops.append(top)
        totals.append(jnp.sum(w, axis=1, keepdims=True) + w_new)
        news.append(w_new.astype(BF).astype(F32) * new_ref[1, b : b + 1].astype(F32))
    acc = dot(jnp.concatenate(weights, axis=0), own_ref[1], 1, 0)
    acc_ref[...] = acc + jnp.concatenate(news, axis=0)
    top_ref[...] = jnp.broadcast_to(jnp.concatenate(tops, axis=0), (QROWS, HD))
    total_ref[...] = jnp.broadcast_to(jnp.concatenate(totals, axis=0), (QROWS, HD))


def own_part(pages, own_len, q, new_kv, own_kv):
    smem = pl.BlockSpec(memory_space=pltpu.SMEM)
    vmem = pl.BlockSpec(memory_space=pltpu.VMEM)
    return pl.pallas_call(
        own_kernel,
        out_shape=[jax.ShapeDtypeStruct((QROWS, HD), F32)] * 3,
        in_specs=[smem, smem, vmem, vmem, vmem],
        out_specs=[vmem] * 3,
        compiler_params=pltpu.CompilerParams(vmem_limit_bytes=32 << 20),
        name="own_attention",
    )(pages, own_len, q, new_kv, own_kv)


def man_kernel(q_ref, kv_ref, out_ref):
    keys = jnp.concatenate([kv_ref[i, 0] for i in range(4)], axis=0)
    values = jnp.concatenate([kv_ref[i, 1] for i in range(4)], axis=0)
    row = lax.broadcasted_iota(jnp.int32, (STATS, HD), 0)
    for chunk in range(PEERS * QROWS // HD):
        s = dot(keys, q_ref[chunk * HD : (chunk + 1) * HD], 1, 1) * SCALE
        top = jnp.max(s, axis=0, keepdims=True).astype(BF).astype(F32)
        w = jnp.exp(s - top)
        total = jnp.sum(w, axis=0, keepdims=True)
        high = total.astype(BF).astype(F32)
        acc = dot(w.astype(BF), values, 0, 0).astype(BF)
        stats = jnp.where(row == 0, top, jnp.where(row == 1, high, jnp.where(row == 2, total - high, 0.0)))
        stats = stats.astype(BF)
        for j in range(HD // QROWS):
            to = chunk * (HD // QROWS) + j
            out_ref[to, 0:QROWS] = acc[j * QROWS : (j + 1) * QROWS]
            out_ref[to, QROWS : QROWS + STATS] = stats


def man_part(q_all, kv):
    vmem = pl.BlockSpec(memory_space=pltpu.VMEM)
    return pl.pallas_call(
        man_kernel,
        out_shape=jax.ShapeDtypeStruct((PEERS, QROWS + STATS, HD), BF),
        in_specs=[vmem, vmem],
        out_specs=vmem,
        compiler_params=pltpu.CompilerParams(vmem_limit_bytes=32 << 20),
        name="manifest_attention",
    )(q_all, kv)


def join_kernel(place_ref, parts_ref, acc_ref, top_ref, total_ref, out_ref, rows_ref):
    stats = parts_ref[:, QROWS : QROWS + STATS, :].reshape(PEERS * STATS, HD)
    lane = lax.broadcasted_iota(jnp.int32, (QROWS, HD), 1)
    row = lax.broadcasted_iota(jnp.int32, (QROWS, HD), 0)
    pick = jnp.where(lane == row + place_ref[0] * QROWS, 1.0, 0.0).astype(BF)
    s = dot(pick, stats, 1, 1)
    n = PEERS * STATS
    kind = lax.broadcasted_iota(jnp.int32, (QROWS, n), 1) % STATS
    totals = pltpu.roll(s, n - 1, 1) + pltpu.roll(s, n - 2, 1)
    own_top = top_ref[:, 0:1]
    top = jnp.maximum(jnp.max(jnp.where(kind == 0, s, -jnp.inf), axis=1, keepdims=True), own_top)
    factor = jnp.where(kind == 0, jnp.exp(jnp.minimum(s - top, 0.0)), 0.0)
    own_factor = jnp.exp(own_top - top)
    total = jnp.sum(factor * totals, axis=1, keepdims=True) + own_factor * total_ref[:, 0:1]
    acc = own_factor * acc_ref[...]
    for i in range(PEERS):
        acc = acc + factor[:, i * STATS : i * STATS + 1] * parts_ref[i, 0:QROWS].astype(F32)
    rows_ref[...] = acc / total
    for h in range(GROUP):
        rows = rows_ref[pl.ds(h, ROWS, stride=GROUP), :].astype(BF)
        for i in range(CHIPS):
            out_ref[i, :, h * HD : (h + 1) * HD] = rows


def join_part(place, parts, acc, top, total):
    smem = pl.BlockSpec(memory_space=pltpu.SMEM)
    vmem = pl.BlockSpec(memory_space=pltpu.VMEM)
    return pl.pallas_call(
        join_kernel,
        out_shape=jax.ShapeDtypeStruct((CHIPS, ROWS, GROUP * HD), BF),
        in_specs=[smem, vmem, vmem, vmem, vmem],
        out_specs=vmem,
        scratch_shapes=[pltpu.VMEM((QROWS, HD), F32)],
        compiler_params=pltpu.CompilerParams(vmem_limit_bytes=32 << 20),
        name="join_attention",
    )(place, parts, acc, top, total)


def project_kernel(x_ref, w0_ref, w1_ref, out_ref):
    w = jnp.concatenate([w0_ref[...], w1_ref[...]], axis=1)
    y = dot(x_ref[...], w, 1, 0).astype(BF)
    for i in range(8):
        out_ref[i] = y


def mlp_kernel(x_ref, g0_ref, g1_ref, u0_ref, u1_ref, out_ref):
    x = x_ref[...]
    gate = dot(x, jnp.concatenate([g0_ref[...], g1_ref[...]], axis=0), 1, 0)
    up = dot(x, jnp.concatenate([u0_ref[...], u1_ref[...]], axis=0), 1, 0)
    for j in range(CHIPS):
        at = slice(j * ROWS, (j + 1) * ROWS)
        out_ref[j] = jnp.concatenate([gate[at], up[at]], axis=0).astype(BF)


def dense(kernel, name, out_shape, *args):
    vmem = pl.BlockSpec(memory_space=pltpu.VMEM)
    return pl.pallas_call(
        kernel,
        out_shape=jax.ShapeDtypeStruct(out_shape, BF),
        in_specs=[vmem] * len(args),
        out_specs=vmem,
        compiler_params=pltpu.CompilerParams(vmem_limit_bytes=40 << 20),
        name=name,
    )(*args)


def swap(x):
    return lax.ppermute(x, "c", [(0, 1), (1, 0)])


def exchange(x, axes):
    return lax.all_to_all(x, axes, 0, 0, tiled=True)


def on_device(queries, new_kv, own_kv, man_kv, pages, own_len, resid, w_out, w_gate, w_up):
    core = lax.axis_index("c")
    tie = lax.optimization_barrier
    width = w_gate.shape[1]
    rows = CHIPS * ROWS
    q = queries.reshape(QROWS, HD)
    q_all = exchange(jnp.broadcast_to(q[None], (PEERS, QROWS, HD)), SPARSE).reshape(PEERS * QROWS, HD)
    kv = lax.all_gather(man_kv.reshape(1, 2, 2 * PAGE, HD), ("p", "c"), axis=0, tiled=True)
    parts = exchange(man_part(q_all, kv), SPARSE)
    own = own_part(pages, own_len, q, new_kv, own_kv.reshape(2, POOL * PAGE, HD))
    parts, own, w_out_c = tie((parts, own, swap(w_out)))
    place = (lax.axis_index(SPARSE) % 4).astype(jnp.int32).reshape(1)
    attn = exchange(join_part(place, parts, *own), PLANE).reshape(rows, GROUP * HD)
    res = resid.reshape(CHIPS, 2, ROWS, HD)
    mine = jnp.where(core == 0, res[:, 0], res[:, 1])
    theirs = swap(jnp.where(core == 0, res[:, 1], res[:, 0]))
    res = jnp.concatenate([mine, theirs], axis=-1).reshape(rows, 2 * HD).astype(F32)
    attn, w_gate_c, w_up_c, res = tie((attn, swap(w_gate), swap(w_up), res))

    heads = exchange(dense(project_kernel, "project", (8, rows, 2 * HD), attn, w_out, w_out_c), HEAD)
    out2 = (res + heads.astype(F32).sum(0)).astype(BF)
    both = dense(mlp_kernel, "gate_up", (CHIPS, 2 * ROWS, width), out2, w_gate, w_gate_c, w_up, w_up_c)
    joined = exchange(both, PLANE).astype(F32).sum(0)
    hidden = (jax.nn.silu(joined[:ROWS]) * joined[ROWS:]).astype(BF)

    kept = out2[:, :HD].reshape(CHIPS, 1, ROWS, HD)
    given = swap(out2[:, HD:]).reshape(CHIPS, 1, ROWS, HD)
    first = jnp.where(core == 0, kept, given)
    second = jnp.where(core == 0, given, kept)
    resid_out = jnp.concatenate([first, second], axis=1).reshape(CHIPS * 2 * ROWS, HD)
    return (resid_out, hidden)


def solution(mesh):
    fine = Mesh(mesh.devices.reshape(8, 2, 2, 2, 2, 4), ("y", "zq", "p", "c", "zh", "x"))
    in_specs = (
        P(REQ, HEAD),
        P(None, REQ, HEAD),
        P(None, REQ, None, HEAD),
        P(None, REQ, None, HEAD),
        P(REQ, None),
        P(REQ),
        P(None, REQ),
        P(HEAD, REQ),
        P(REQ, HEAD),
        P(REQ, HEAD),
    )
    out_specs = (P(None, REQ), P(REQ, HEAD))
    return jax.shard_map(
        on_device, mesh=fine, in_specs=in_specs, out_specs=out_specs, check_vma=False
    )
```

```python
import jax
import jax.numpy as jnp
from jax import lax
from jax.experimental import pallas as pl
from jax.experimental.pallas import tpu as pltpu
from jax.sharding import Mesh, PartitionSpec as P

HD = 128
PAGE = 64
MAXP = 8
GROUP = 8
ROWS = 4
QROWS = ROWS * GROUP
POOL = 32
CHIPS = 32
PEERS = 16
STATS = 8
SCALE = HD**-0.5
PLANE = ("y", "zq", "p")
SPARSE = ("y", "zq")
HEAD = ("zh", "x")
REQ = ("y", "zq", "p", "c")
BF = jnp.bfloat16
F32 = jnp.float32


def dot(a, b, ca, cb):
    return lax.dot_general(a, b, (((ca,), (cb,)), ((), ())), preferred_element_type=F32)


def own_kernel(pages_ref, len_ref, q_ref, new_ref, own_ref, acc_ref, top_ref, total_ref):
    tokens = POOL * PAGE
    scores = dot(q_ref[...], own_ref[0], 1, 1) * SCALE
    page_of = lax.broadcasted_iota(jnp.int32, (GROUP, tokens), 1) // PAGE
    weights, tops, totals, news = [], [], [], []
    for b in range(ROWS):
        count = jnp.zeros((GROUP, tokens), F32)
        for i in range(MAXP):
            page = jnp.where(i < len_ref[b], pages_ref[b, i], -1)
            count = count + jnp.where(page_of == page, 1.0, 0.0)
        s = jnp.where(count > 0.0, scores[b * GROUP : (b + 1) * GROUP], -jnp.inf)
        q = q_ref[b * GROUP : (b + 1) * GROUP].astype(F32)
        s_new = jnp.sum(q * new_ref[0, b : b + 1].astype(F32), axis=1, keepdims=True) * SCALE
        top = jnp.maximum(jnp.max(s, axis=1, keepdims=True), s_new)
        w = jnp.exp(s - top) * count
        w_new = jnp.exp(s_new - top)
        weights.append(w.astype(BF))
        tops.append(top)
        totals.append(jnp.sum(w, axis=1, keepdims=True) + w_new)
        news.append(w_new.astype(BF).astype(F32) * new_ref[1, b : b + 1].astype(F32))
    acc = dot(jnp.concatenate(weights, axis=0), own_ref[1], 1, 0)
    acc_ref[...] = acc + jnp.concatenate(news, axis=0)
    top_ref[...] = jnp.broadcast_to(jnp.concatenate(tops, axis=0), (QROWS, HD))
    total_ref[...] = jnp.broadcast_to(jnp.concatenate(totals, axis=0), (QROWS, HD))


def own_part(pages, own_len, q, new_kv, own_kv):
    smem = pl.BlockSpec(memory_space=pltpu.SMEM)
    vmem = pl.BlockSpec(memory_space=pltpu.VMEM)
    return pl.pallas_call(
        own_kernel,
        out_shape=[jax.ShapeDtypeStruct((QROWS, HD), F32)] * 3,
        in_specs=[smem, smem, vmem, vmem, vmem],
        out_specs=[vmem] * 3,
        compiler_params=pltpu.CompilerParams(vmem_limit_bytes=32 << 20),
        name="own_attention",
    )(pages, own_len, q, new_kv, own_kv)


def man_kernel(q_ref, kv_ref, out_ref):
    keys = jnp.concatenate([kv_ref[i, 0] for i in range(4)], axis=0)
    values = jnp.concatenate([kv_ref[i, 1] for i in range(4)], axis=0)
    row = lax.broadcasted_iota(jnp.int32, (STATS, HD), 0)
    for chunk in range(PEERS * QROWS // HD):
        s = dot(keys, q_ref[chunk * HD : (chunk + 1) * HD], 1, 1) * SCALE
        top = jnp.max(s, axis=0, keepdims=True).astype(BF).astype(F32)
        w = jnp.exp(s - top)
        total = jnp.sum(w, axis=0, keepdims=True)
        high = total.astype(BF).astype(F32)
        acc = dot(w.astype(BF), values, 0, 0).astype(BF)
        stats = jnp.where(row == 0, top, jnp.where(row == 1, high, jnp.where(row == 2, total - high, 0.0)))
        stats = stats.astype(BF)
        for j in range(HD // QROWS):
            to = chunk * (HD // QROWS) + j
            out_ref[to, 0:QROWS] = acc[j * QROWS : (j + 1) * QROWS]
            out_ref[to, QROWS : QROWS + STATS] = stats


def man_part(q_all, kv):
    vmem = pl.BlockSpec(memory_space=pltpu.VMEM)
    return pl.pallas_call(
        man_kernel,
        out_shape=jax.ShapeDtypeStruct((PEERS, QROWS + STATS, HD), BF),
        in_specs=[vmem, vmem],
        out_specs=vmem,
        compiler_params=pltpu.CompilerParams(vmem_limit_bytes=32 << 20),
        name="manifest_attention",
    )(q_all, kv)


def join_kernel(place_ref, parts_ref, acc_ref, top_ref, total_ref, out_ref, rows_ref):
    stats = parts_ref[:, QROWS : QROWS + STATS, :].reshape(PEERS * STATS, HD)
    lane = lax.broadcasted_iota(jnp.int32, (QROWS, HD), 1)
    row = lax.broadcasted_iota(jnp.int32, (QROWS, HD), 0)
    pick = jnp.where(lane == row + place_ref[0] * QROWS, 1.0, 0.0).astype(BF)
    s = dot(pick, stats, 1, 1)
    n = PEERS * STATS
    kind = lax.broadcasted_iota(jnp.int32, (QROWS, n), 1) % STATS
    totals = pltpu.roll(s, n - 1, 1) + pltpu.roll(s, n - 2, 1)
    own_top = top_ref[:, 0:1]
    top = jnp.maximum(jnp.max(jnp.where(kind == 0, s, -jnp.inf), axis=1, keepdims=True), own_top)
    factor = jnp.where(kind == 0, jnp.exp(jnp.minimum(s - top, 0.0)), 0.0)
    own_factor = jnp.exp(own_top - top)
    total = jnp.sum(factor * totals, axis=1, keepdims=True) + own_factor * total_ref[:, 0:1]
    acc = own_factor * acc_ref[...]
    for i in range(PEERS):
        acc = acc + factor[:, i * STATS : i * STATS + 1] * parts_ref[i, 0:QROWS].astype(F32)
    rows_ref[...] = acc / total
    for h in range(GROUP):
        rows = rows_ref[pl.ds(h, ROWS, stride=GROUP), :].astype(BF)
        for i in range(CHIPS):
            out_ref[i, :, h * HD : (h + 1) * HD] = rows


def join_part(place, parts, acc, top, total):
    smem = pl.BlockSpec(memory_space=pltpu.SMEM)
    vmem = pl.BlockSpec(memory_space=pltpu.VMEM)
    return pl.pallas_call(
        join_kernel,
        out_shape=jax.ShapeDtypeStruct((CHIPS, ROWS, GROUP * HD), BF),
        in_specs=[smem, vmem, vmem, vmem, vmem],
        out_specs=vmem,
        scratch_shapes=[pltpu.VMEM((QROWS, HD), F32)],
        compiler_params=pltpu.CompilerParams(vmem_limit_bytes=32 << 20),
        name="join_attention",
    )(place, parts, acc, top, total)


def project_kernel(x_ref, w0_ref, w1_ref, out_ref):
    w = jnp.concatenate([w0_ref[...], w1_ref[...]], axis=1)
    out_ref[...] = dot(x_ref[...], w, 1, 0).astype(BF)


def add_kernel(a_ref, b_ref, out_ref):
    block = (a_ref[...].astype(F32) + b_ref[...].astype(F32)).astype(BF)
    for i in range(4):
        out_ref[i] = block


def mlp_kernel(x_ref, g0_ref, g1_ref, u0_ref, u1_ref, out_ref):
    x = x_ref[...]
    gate = dot(x, jnp.concatenate([g0_ref[...], g1_ref[...]], axis=0), 1, 0)
    up = dot(x, jnp.concatenate([u0_ref[...], u1_ref[...]], axis=0), 1, 0)
    for j in range(CHIPS):
        at = slice(j * ROWS, (j + 1) * ROWS)
        out_ref[j] = jnp.concatenate([gate[at], up[at]], axis=0).astype(BF)


def dense(kernel, name, out_shape, *args):
    vmem = pl.BlockSpec(memory_space=pltpu.VMEM)
    return pl.pallas_call(
        kernel,
        out_shape=jax.ShapeDtypeStruct(out_shape, BF),
        in_specs=[vmem] * len(args),
        out_specs=vmem,
        compiler_params=pltpu.CompilerParams(vmem_limit_bytes=40 << 20),
        name=name,
    )(*args)


def swap(x):
    return lax.ppermute(x, "c", [(0, 1), (1, 0)])


def exchange(x, axes):
    return lax.all_to_all(x, axes, 0, 0, tiled=True)


def on_device(queries, new_kv, own_kv, man_kv, pages, own_len, resid, w_out, w_gate, w_up):
    core = lax.axis_index("c")
    tie = lax.optimization_barrier
    width = w_gate.shape[1]
    rows = CHIPS * ROWS
    q = queries.reshape(QROWS, HD)
    q_all = exchange(jnp.broadcast_to(q[None], (PEERS, QROWS, HD)), SPARSE).reshape(PEERS * QROWS, HD)
    kv = lax.all_gather(man_kv.reshape(1, 2, 2 * PAGE, HD), ("p", "c"), axis=0, tiled=True)
    parts = exchange(man_part(q_all, kv), SPARSE)
    own = own_part(pages, own_len, q, new_kv, own_kv.reshape(2, POOL * PAGE, HD))
    parts, own, w_out_c = tie((parts, own, swap(w_out)))
    place = (lax.axis_index(SPARSE) % 4).astype(jnp.int32).reshape(1)
    attn = exchange(join_part(place, parts, *own), PLANE).reshape(rows, GROUP * HD)
    res = resid.reshape(CHIPS, 2, ROWS, HD)
    mine = jnp.where(core == 0, res[:, 0], res[:, 1])
    theirs = swap(jnp.where(core == 0, res[:, 1], res[:, 0]))
    res = jnp.concatenate([mine, theirs], axis=-1).reshape(rows, 2 * HD).astype(F32)
    attn, w_gate_c, w_up_c, res = tie((attn, swap(w_gate), swap(w_up), res))

    share = dense(project_kernel, "project", (rows, 2 * HD), attn, w_out, w_out_c)
    share2 = lax.ppermute(share, "zh", [(0, 1), (1, 0)])
    heads = exchange(dense(add_kernel, "add_shares", (4, rows, 2 * HD), share, share2), "x")
    out2 = (res + heads.astype(F32).sum(0)).astype(BF)
    both = dense(mlp_kernel, "gate_up", (CHIPS, 2 * ROWS, width), out2, w_gate, w_gate_c, w_up, w_up_c)
    joined = exchange(both, PLANE).astype(F32).sum(0)
    hidden = (jax.nn.silu(joined[:ROWS]) * joined[ROWS:]).astype(BF)

    kept = out2[:, :HD].reshape(CHIPS, 1, ROWS, HD)
    given = swap(out2[:, HD:]).reshape(CHIPS, 1, ROWS, HD)
    first = jnp.where(core == 0, kept, given)
    second = jnp.where(core == 0, given, kept)
    resid_out = jnp.concatenate([first, second], axis=1).reshape(CHIPS * 2 * ROWS, HD)
    return (resid_out, hidden)


def solution(mesh):
    fine = Mesh(mesh.devices.reshape(8, 2, 2, 2, 2, 4), ("y", "zq", "p", "c", "zh", "x"))
    in_specs = (
        P(REQ, HEAD),
        P(None, REQ, HEAD),
        P(None, REQ, None, HEAD),
        P(None, REQ, None, HEAD),
        P(REQ, None),
        P(REQ),
        P(None, REQ),
        P(HEAD, REQ),
        P(REQ, HEAD),
        P(REQ, HEAD),
    )
    out_specs = (P(None, REQ), P(REQ, HEAD))
    return jax.shard_map(
        on_device, mesh=fine, in_specs=in_specs, out_specs=out_specs, check_vma=False
    )
```

```python
import jax
import jax.numpy as jnp
from jax import lax
from jax.experimental import pallas as pl
from jax.experimental.pallas import tpu as pltpu
from jax.sharding import Mesh, PartitionSpec as P

HD = 128
PAGE = 64
MAXP = 8
GROUP = 8
ROWS = 4
QROWS = ROWS * GROUP
POOL = 32
PEERS = 16
STATS = 8
SCALE = HD**-0.5
SPARSE = ("y", "zq")
HEAD = ("zh", "x")
REQ = ("y", "zq", "p", "c")
BF = jnp.bfloat16
F32 = jnp.float32


def dot(a, b, ca, cb):
    return lax.dot_general(a, b, (((ca,), (cb,)), ((), ())), preferred_element_type=F32)


def own_kernel(pages_ref, len_ref, q_ref, new_ref, own_ref, acc_ref, top_ref, total_ref):
    tokens = POOL * PAGE
    scores = dot(q_ref[...], own_ref[0], 1, 1) * SCALE
    page_of = lax.broadcasted_iota(jnp.int32, (GROUP, tokens), 1) // PAGE
    weights, tops, totals, news = [], [], [], []
    for b in range(ROWS):
        count = jnp.zeros((GROUP, tokens), F32)
        for i in range(MAXP):
            page = jnp.where(i < len_ref[b], pages_ref[b, i], -1)
            count = count + jnp.where(page_of == page, 1.0, 0.0)
        s = jnp.where(count > 0.0, scores[b * GROUP : (b + 1) * GROUP], -jnp.inf)
        q = q_ref[b * GROUP : (b + 1) * GROUP].astype(F32)
        s_new = jnp.sum(q * new_ref[0, b : b + 1].astype(F32), axis=1, keepdims=True) * SCALE
        top = jnp.maximum(jnp.max(s, axis=1, keepdims=True), s_new)
        w = jnp.exp(s - top) * count
        w_new = jnp.exp(s_new - top)
        weights.append(w.astype(BF))
        tops.append(top)
        totals.append(jnp.sum(w, axis=1, keepdims=True) + w_new)
        news.append(w_new.astype(BF).astype(F32) * new_ref[1, b : b + 1].astype(F32))
    acc = dot(jnp.concatenate(weights, axis=0), own_ref[1], 1, 0)
    acc_ref[...] = acc + jnp.concatenate(news, axis=0)
    top_ref[...] = jnp.broadcast_to(jnp.concatenate(tops, axis=0), (QROWS, HD))
    total_ref[...] = jnp.broadcast_to(jnp.concatenate(totals, axis=0), (QROWS, HD))


def own_part(pages, own_len, q, new_kv, own_kv):
    smem = pl.BlockSpec(memory_space=pltpu.SMEM)
    vmem = pl.BlockSpec(memory_space=pltpu.VMEM)
    return pl.pallas_call(
        own_kernel,
        out_shape=[jax.ShapeDtypeStruct((QROWS, HD), F32)] * 3,
        in_specs=[smem, smem, vmem, vmem, vmem],
        out_specs=[vmem] * 3,
        compiler_params=pltpu.CompilerParams(vmem_limit_bytes=32 << 20),
        name="own_attention",
    )(pages, own_len, q, new_kv, own_kv)


def man_kernel(q_ref, kv_ref, out_ref):
    keys = jnp.concatenate([kv_ref[i, 0] for i in range(4)], axis=0)
    values = jnp.concatenate([kv_ref[i, 1] for i in range(4)], axis=0)
    row = lax.broadcasted_iota(jnp.int32, (STATS, HD), 0)
    for chunk in range(PEERS * QROWS // HD):
        s = dot(keys, q_ref[chunk * HD : (chunk + 1) * HD], 1, 1) * SCALE
        top = jnp.max(s, axis=0, keepdims=True).astype(BF).astype(F32)
        w = jnp.exp(s - top)
        total = jnp.sum(w, axis=0, keepdims=True)
        high = total.astype(BF).astype(F32)
        acc = dot(w.astype(BF), values, 0, 0).astype(BF)
        stats = jnp.where(row == 0, top, jnp.where(row == 1, high, jnp.where(row == 2, total - high, 0.0)))
        stats = stats.astype(BF)
        for j in range(HD // QROWS):
            to = chunk * (HD // QROWS) + j
            out_ref[to, 0:QROWS] = acc[j * QROWS : (j + 1) * QROWS]
            out_ref[to, QROWS : QROWS + STATS] = stats


def man_part(q_all, kv):
    vmem = pl.BlockSpec(memory_space=pltpu.VMEM)
    return pl.pallas_call(
        man_kernel,
        out_shape=jax.ShapeDtypeStruct((PEERS, QROWS + STATS, HD), BF),
        in_specs=[vmem, vmem],
        out_specs=vmem,
        compiler_params=pltpu.CompilerParams(vmem_limit_bytes=32 << 20),
        name="manifest_attention",
    )(q_all, kv)


def join_kernel(place_ref, parts_ref, acc_ref, top_ref, total_ref, out_ref, rows_ref):
    stats = parts_ref[:, QROWS : QROWS + STATS, :].reshape(PEERS * STATS, HD)
    lane = lax.broadcasted_iota(jnp.int32, (QROWS, HD), 1)
    row = lax.broadcasted_iota(jnp.int32, (QROWS, HD), 0)
    pick = jnp.where(lane == row + place_ref[0] * QROWS, 1.0, 0.0).astype(BF)
    s = dot(pick, stats, 1, 1)
    n = PEERS * STATS
    kind = lax.broadcasted_iota(jnp.int32, (QROWS, n), 1) % STATS
    totals = pltpu.roll(s, n - 1, 1) + pltpu.roll(s, n - 2, 1)
    own_top = top_ref[:, 0:1]
    top = jnp.maximum(jnp.max(jnp.where(kind == 0, s, -jnp.inf), axis=1, keepdims=True), own_top)
    factor = jnp.where(kind == 0, jnp.exp(jnp.minimum(s - top, 0.0)), 0.0)
    own_factor = jnp.exp(own_top - top)
    total = jnp.sum(factor * totals, axis=1, keepdims=True) + own_factor * total_ref[:, 0:1]
    acc = own_factor * acc_ref[...]
    for i in range(PEERS):
        acc = acc + factor[:, i * STATS : i * STATS + 1] * parts_ref[i, 0:QROWS].astype(F32)
    rows_ref[...] = acc / total
    for h in range(GROUP):
        rows = rows_ref[pl.ds(h, ROWS, stride=GROUP), :].astype(BF)
        for i in range(PEERS):
            out_ref[i, :, h * HD : (h + 1) * HD] = rows


def join_part(place, parts, acc, top, total):
    smem = pl.BlockSpec(memory_space=pltpu.SMEM)
    vmem = pl.BlockSpec(memory_space=pltpu.VMEM)
    return pl.pallas_call(
        join_kernel,
        out_shape=jax.ShapeDtypeStruct((PEERS, ROWS, GROUP * HD), BF),
        in_specs=[smem, vmem, vmem, vmem, vmem],
        out_specs=vmem,
        scratch_shapes=[pltpu.VMEM((QROWS, HD), F32)],
        compiler_params=pltpu.CompilerParams(vmem_limit_bytes=32 << 20),
        name="join_attention",
    )(place, parts, acc, top, total)


def project_kernel(x_ref, w0_ref, w1_ref, w2_ref, w3_ref, out_ref):
    x = x_ref[...]
    for k in range(2):
        w = [w_ref[0 : GROUP * HD] for w_ref in ((w0_ref, w1_ref), (w2_ref, w3_ref))[k]]
        out_ref[:, 2 * k * HD : 2 * (k + 1) * HD] = dot(x, jnp.concatenate(w, axis=1), 1, 0).astype(BF)


def add_kernel(a_ref, b_ref, out_ref):
    block = (a_ref[...].astype(F32) + b_ref[...].astype(F32)).astype(BF)
    for i in range(4):
        out_ref[i] = block


def mlp_kernel(x_ref, w0_ref, w1_ref, w2_ref, w3_ref, out_ref):
    low, high = x_ref[:, 0 : 2 * HD], x_ref[:, 2 * HD :]

    def product(k):
        w = [w_ref[k * HD : (k + 1) * HD] for w_ref in (w0_ref, w1_ref, w2_ref, w3_ref)]
        return dot(low, jnp.concatenate(w[:2], axis=0), 1, 0) + dot(high, jnp.concatenate(w[2:], axis=0), 1, 0)

    gate, up = product(0), product(1)
    for j in range(PEERS):
        at = slice(j * ROWS, (j + 1) * ROWS)
        out_ref[j] = jnp.concatenate([gate[at], up[at]], axis=0).astype(BF)


def dense(kernel, name, out_shape, *args):
    vmem = pl.BlockSpec(memory_space=pltpu.VMEM)
    return pl.pallas_call(
        kernel,
        out_shape=jax.ShapeDtypeStruct(out_shape, BF),
        in_specs=[vmem] * len(args),
        out_specs=vmem,
        compiler_params=pltpu.CompilerParams(vmem_limit_bytes=40 << 20),
        name=name,
    )(*args)


def swap(x):
    return lax.ppermute(x, "c", [(0, 1), (1, 0)])


def pair(x):
    return lax.ppermute(x, "p", [(0, 1), (1, 0)])


def exchange(x, axes):
    return lax.all_to_all(x, axes, 0, 0, tiled=True)


def pick(x, index, axis):
    return jnp.where(index == 0, lax.index_in_dim(x, 0, axis, False), lax.index_in_dim(x, 1, axis, False))


def ordered(own, other, index, axis):
    return jnp.where(index == 0, jnp.stack([own, other], axis), jnp.stack([other, own], axis))


def on_device(queries, new_kv, own_kv, man_kv, pages, own_len, resid, w_out, w_gate, w_up):
    core, side = lax.axis_index("c"), lax.axis_index("p")
    tie = lax.optimization_barrier
    width = w_gate.shape[1]
    rows = PEERS * ROWS
    q = queries.reshape(QROWS, HD)
    q_all = exchange(jnp.broadcast_to(q[None], (PEERS, QROWS, HD)), SPARSE).reshape(PEERS * QROWS, HD)
    kv = lax.all_gather(man_kv.reshape(1, 2, 2 * PAGE, HD), ("p", "c"), axis=0, tiled=True)
    parts = exchange(man_part(q_all, kv), SPARSE)
    own = own_part(pages, own_len, q, new_kv, own_kv.reshape(2, POOL * PAGE, HD))
    out_w = jnp.concatenate([w_out, resid], axis=0)
    parts, own, out_w_c, out_w_p = tie((parts, own, swap(out_w), pair(out_w)))
    place = (lax.axis_index(SPARSE) % 4).astype(jnp.int32).reshape(1)
    attn = exchange(join_part(place, parts, *own), SPARSE).reshape(rows, GROUP * HD)
    mlp_w = jnp.concatenate([w_gate, w_up], axis=0)
    mlp_w_p = pair(mlp_w)
    attn, out_w_pc, mlp_w_p = tie((attn, swap(out_w_p), mlp_w_p))
    out_ws = (out_w, out_w_c, out_w_p, out_w_pc)
    res = [pick(pick(w[GROUP * HD :].reshape(PEERS, 2, 2, ROWS, HD), side, 1), core, 1) for w in out_ws]
    res = jnp.concatenate(res, axis=-1).reshape(rows, 4 * HD).astype(F32)

    share = dense(project_kernel, "project", (rows, 4 * HD), attn, *out_ws)
    share2 = lax.ppermute(share, "zh", [(0, 1), (1, 0)])
    heads = exchange(dense(add_kernel, "add_shares", (4, rows, 4 * HD), share, share2), "x")
    out4 = (res + heads.astype(F32).sum(0)).astype(BF)
    both = dense(
        mlp_kernel, "gate_up", (PEERS, 2 * ROWS, width), out4, mlp_w, swap(mlp_w), mlp_w_p, swap(mlp_w_p)
    )
    joined = exchange(both, SPARSE).astype(F32).sum(0)
    hidden = (jax.nn.silu(joined[:ROWS]) * joined[ROWS:]).astype(BF)

    out = out4.reshape(PEERS, ROWS, 2, 2, HD)
    out = ordered(out[:, :, 0], pair(out[:, :, 1]), side, 1)
    out = ordered(out[:, :, :, 0], swap(out[:, :, :, 1]), core, 2)
    return (out.reshape(PEERS * 4 * ROWS, HD), hidden)


def solution(mesh):
    fine = Mesh(mesh.devices.reshape(8, 2, 2, 2, 2, 4), ("y", "zq", "p", "c", "zh", "x"))
    in_specs = (
        P(REQ, HEAD),
        P(None, REQ, HEAD),
        P(None, REQ, None, HEAD),
        P(None, REQ, None, HEAD),
        P(REQ, None),
        P(REQ),
        P(None, REQ),
        P(HEAD, REQ),
        P(REQ, HEAD),
        P(REQ, HEAD),
    )
    out_specs = (P(None, REQ), P(REQ, HEAD))
    return jax.shard_map(
        on_device, mesh=fine, in_specs=in_specs, out_specs=out_specs, check_vma=False
    )
```

```python
import jax
import jax.numpy as jnp
from jax import lax
from jax.experimental import pallas as pl
from jax.experimental.pallas import tpu as pltpu
from jax.sharding import Mesh, PartitionSpec as P

HD = 128
PAGE = 64
MAXP = 8
GROUP = 8
ROWS = 4
QROWS = ROWS * GROUP
POOL = 32
PEERS = 16
STATS = 8
SCALE = HD**-0.5
SPARSE = ("y", "zq")
HEAD = ("zh", "x")
REQ = ("y", "zq", "p", "c")
BF = jnp.bfloat16
F32 = jnp.float32


def dot(a, b, ca, cb):
    return lax.dot_general(a, b, (((ca,), (cb,)), ((), ())), preferred_element_type=F32)


def own_kernel(pages_ref, len_ref, q_ref, new_ref, own_ref, acc_ref, top_ref, total_ref):
    tokens = POOL * PAGE
    scores = dot(q_ref[...], own_ref[0], 1, 1) * SCALE
    page_of = lax.broadcasted_iota(jnp.int32, (GROUP, tokens), 1) // PAGE
    weights, tops, totals, news = [], [], [], []
    for b in range(ROWS):
        count = jnp.zeros((GROUP, tokens), F32)
        for i in range(MAXP):
            page = jnp.where(i < len_ref[b], pages_ref[b, i], -1)
            count = count + jnp.where(page_of == page, 1.0, 0.0)
        s = jnp.where(count > 0.0, scores[b * GROUP : (b + 1) * GROUP], -jnp.inf)
        q = q_ref[b * GROUP : (b + 1) * GROUP].astype(F32)
        s_new = jnp.sum(q * new_ref[0, b : b + 1].astype(F32), axis=1, keepdims=True) * SCALE
        top = jnp.maximum(jnp.max(s, axis=1, keepdims=True), s_new)
        w = jnp.exp(s - top) * count
        w_new = jnp.exp(s_new - top)
        weights.append(w.astype(BF))
        tops.append(top)
        totals.append(jnp.sum(w, axis=1, keepdims=True) + w_new)
        news.append(w_new.astype(BF).astype(F32) * new_ref[1, b : b + 1].astype(F32))
    acc = dot(jnp.concatenate(weights, axis=0), own_ref[1], 1, 0)
    acc_ref[...] = acc + jnp.concatenate(news, axis=0)
    top_ref[...] = jnp.broadcast_to(jnp.concatenate(tops, axis=0), (QROWS, HD))
    total_ref[...] = jnp.broadcast_to(jnp.concatenate(totals, axis=0), (QROWS, HD))


def own_part(pages, own_len, q, new_kv, own_kv):
    smem = pl.BlockSpec(memory_space=pltpu.SMEM)
    vmem = pl.BlockSpec(memory_space=pltpu.VMEM)
    return pl.pallas_call(
        own_kernel,
        out_shape=[jax.ShapeDtypeStruct((QROWS, HD), F32)] * 3,
        in_specs=[smem, smem, vmem, vmem, vmem],
        out_specs=[vmem] * 3,
        compiler_params=pltpu.CompilerParams(vmem_limit_bytes=32 << 20),
        name="own_attention",
    )(pages, own_len, q, new_kv, own_kv)


def man_kernel(q_ref, kv_ref, out_ref):
    keys = jnp.concatenate([kv_ref[i, 0] for i in range(4)], axis=0)
    values = jnp.concatenate([kv_ref[i, 1] for i in range(4)], axis=0)
    row = lax.broadcasted_iota(jnp.int32, (STATS, HD), 0)
    for chunk in range(PEERS * QROWS // HD):
        s = dot(keys, q_ref[chunk * HD : (chunk + 1) * HD], 1, 1) * SCALE
        top = jnp.max(s, axis=0, keepdims=True).astype(BF).astype(F32)
        w = jnp.exp(s - top)
        total = jnp.sum(w, axis=0, keepdims=True)
        high = total.astype(BF).astype(F32)
        acc = dot(w.astype(BF), values, 0, 0).astype(BF)
        stats = jnp.where(row == 0, top, jnp.where(row == 1, high, jnp.where(row == 2, total - high, 0.0)))
        stats = stats.astype(BF)
        for j in range(HD // QROWS):
            to = chunk * (HD // QROWS) + j
            out_ref[to, 0:QROWS] = acc[j * QROWS : (j + 1) * QROWS]
            out_ref[to, QROWS : QROWS + STATS] = stats


def man_part(q_all, kv):
    vmem = pl.BlockSpec(memory_space=pltpu.VMEM)
    return pl.pallas_call(
        man_kernel,
        out_shape=jax.ShapeDtypeStruct((PEERS, QROWS + STATS, HD), BF),
        in_specs=[vmem, vmem],
        out_specs=vmem,
        compiler_params=pltpu.CompilerParams(vmem_limit_bytes=32 << 20),
        name="manifest_attention",
    )(q_all, kv)


def join_kernel(place_ref, parts_ref, acc_ref, top_ref, total_ref, out_ref, rows_ref):
    stats = parts_ref[:, QROWS : QROWS + STATS, :].reshape(PEERS * STATS, HD)
    lane = lax.broadcasted_iota(jnp.int32, (QROWS, HD), 1)
    row = lax.broadcasted_iota(jnp.int32, (QROWS, HD), 0)
    pick = jnp.where(lane == row + place_ref[0] * QROWS, 1.0, 0.0).astype(BF)
    s = dot(pick, stats, 1, 1)
    n = PEERS * STATS
    kind = lax.broadcasted_iota(jnp.int32, (QROWS, n), 1) % STATS
    totals = pltpu.roll(s, n - 1, 1) + pltpu.roll(s, n - 2, 1)
    own_top = top_ref[:, 0:1]
    top = jnp.maximum(jnp.max(jnp.where(kind == 0, s, -jnp.inf), axis=1, keepdims=True), own_top)
    factor = jnp.where(kind == 0, jnp.exp(jnp.minimum(s - top, 0.0)), 0.0)
    own_factor = jnp.exp(own_top - top)
    total = jnp.sum(factor * totals, axis=1, keepdims=True) + own_factor * total_ref[:, 0:1]
    acc = own_factor * acc_ref[...]
    for i in range(PEERS):
        acc = acc + factor[:, i * STATS : i * STATS + 1] * parts_ref[i, 0:QROWS].astype(F32)
    rows_ref[...] = acc / total
    for h in range(GROUP):
        rows = rows_ref[pl.ds(h, ROWS, stride=GROUP), :].astype(BF)
        for i in range(PEERS):
            out_ref[i, :, h * HD : (h + 1) * HD] = rows


def join_part(place, parts, acc, top, total):
    smem = pl.BlockSpec(memory_space=pltpu.SMEM)
    vmem = pl.BlockSpec(memory_space=pltpu.VMEM)
    return pl.pallas_call(
        join_kernel,
        out_shape=jax.ShapeDtypeStruct((PEERS, ROWS, GROUP * HD), BF),
        in_specs=[smem, vmem, vmem, vmem, vmem],
        out_specs=vmem,
        scratch_shapes=[pltpu.VMEM((QROWS, HD), F32)],
        compiler_params=pltpu.CompilerParams(vmem_limit_bytes=32 << 20),
        name="join_attention",
    )(place, parts, acc, top, total)


def project_kernel(x_ref, w0_ref, w1_ref, out_ref):
    x = x_ref[...]
    for k in range(2):
        w = jnp.concatenate([w0_ref[k], w1_ref[k]], axis=1)
        out_ref[:, 2 * k * HD : 2 * (k + 1) * HD] = dot(x, w, 1, 0).astype(BF)


def add_kernel(a_ref, b_ref, out_ref):
    block = (a_ref[...].astype(F32) + b_ref[...].astype(F32)).astype(BF)
    for i in range(4):
        out_ref[i] = block


def mlp_kernel(x_ref, w0_ref, w1_ref, w2_ref, w3_ref, out_ref):
    low, high = x_ref[:, 0 : 2 * HD], x_ref[:, 2 * HD :]

    def product(k):
        w = [w_ref[k * HD : (k + 1) * HD] for w_ref in (w0_ref, w1_ref, w2_ref, w3_ref)]
        return dot(low, jnp.concatenate(w[:2], axis=0), 1, 0) + dot(high, jnp.concatenate(w[2:], axis=0), 1, 0)

    gate, up = product(0), product(1)
    for j in range(PEERS):
        at = slice(j * ROWS, (j + 1) * ROWS)
        out_ref[j] = jnp.concatenate([gate[at], up[at]], axis=0).astype(BF)


def dense(kernel, name, out_shape, *args):
    vmem = pl.BlockSpec(memory_space=pltpu.VMEM)
    return pl.pallas_call(
        kernel,
        out_shape=jax.ShapeDtypeStruct(out_shape, BF),
        in_specs=[vmem] * len(args),
        out_specs=vmem,
        compiler_params=pltpu.CompilerParams(vmem_limit_bytes=40 << 20),
        name=name,
    )(*args)


def swap(x):
    return lax.ppermute(x, "c", [(0, 1), (1, 0)])


def pair(x):
    return lax.ppermute(x, "p", [(0, 1), (1, 0)])


def exchange(x, axes):
    return lax.all_to_all(x, axes, 0, 0, tiled=True)


def pick(x, index, axis):
    return jnp.where(index == 0, lax.index_in_dim(x, 0, axis, False), lax.index_in_dim(x, 1, axis, False))


def ordered(own, other, index, axis):
    return jnp.where(index == 0, jnp.stack([own, other], axis), jnp.stack([other, own], axis))


def on_device(queries, new_kv, own_kv, man_kv, pages, own_len, resid, w_out, w_gate, w_up):
    core, side = lax.axis_index("c"), lax.axis_index("p")
    tie = lax.optimization_barrier
    width = w_gate.shape[1]
    rows = PEERS * ROWS
    q = queries.reshape(QROWS, HD)
    q_all = exchange(jnp.broadcast_to(q[None], (PEERS, QROWS, HD)), SPARSE).reshape(PEERS * QROWS, HD)
    kv = lax.all_gather(man_kv.reshape(1, 2, 2 * PAGE, HD), ("p", "c"), axis=0, tiled=True)
    kv, w_out = tie((kv, w_out))
    parts = exchange(man_part(q_all, kv), SPARSE)
    own = own_part(pages, own_len, q, new_kv, own_kv.reshape(2, POOL * PAGE, HD))
    out_w = w_out
    out_w = jnp.stack([out_w, pair(out_w)])
    parts, own = tie((parts, own))
    place = (lax.axis_index(SPARSE) % 4).astype(jnp.int32).reshape(1)
    attn = exchange(join_part(place, parts, *own), SPARSE).reshape(rows, GROUP * HD)
    mlp_w = jnp.concatenate([w_gate, w_up], axis=0)
    mlp_w_p = pair(mlp_w)
    attn, out_w_c = tie((attn, swap(out_w)))
    out_ws = (out_w, out_w_c)
    share = dense(project_kernel, "project", (rows, 4 * HD), attn, *out_ws)
    share2 = lax.ppermute(share, "zh", [(0, 1), (1, 0)])
    share2, resid = tie((share2, resid))
    res = resid.reshape(PEERS, 2, 2, ROWS, HD)
    res = jnp.stack([pick(res, core, 2), swap(pick(res, 1 - core, 2))], axis=3)
    res = jnp.stack([pick(res, side, 1), pair(pick(res, 1 - side, 1))], axis=2)
    res = res.reshape(rows, 4 * HD).astype(F32)
    heads = exchange(dense(add_kernel, "add_shares", (4, rows, 4 * HD), share, share2), "x")
    out4 = (res + heads.astype(F32).sum(0)).astype(BF)
    both = dense(
        mlp_kernel, "gate_up", (PEERS, 2 * ROWS, width), out4, mlp_w, swap(mlp_w), mlp_w_p, swap(mlp_w_p)
    )
    joined = exchange(both, SPARSE).astype(F32).sum(0)
    hidden = (jax.nn.silu(joined[:ROWS]) * joined[ROWS:]).astype(BF)

    out = out4.reshape(PEERS, ROWS, 2, 2, HD)
    out = ordered(out[:, :, 0], pair(out[:, :, 1]), side, 1)
    out = ordered(out[:, :, :, 0], swap(out[:, :, :, 1]), core, 2)
    return (out.reshape(PEERS * 4 * ROWS, HD), hidden)


def solution(mesh):
    fine = Mesh(mesh.devices.reshape(8, 2, 2, 2, 2, 4), ("y", "zq", "p", "c", "zh", "x"))
    in_specs = (
        P(REQ, HEAD),
        P(None, REQ, HEAD),
        P(None, REQ, None, HEAD),
        P(None, REQ, None, HEAD),
        P(REQ, None),
        P(REQ),
        P(None, REQ),
        P(HEAD, REQ),
        P(REQ, HEAD),
        P(REQ, HEAD),
    )
    out_specs = (P(None, REQ), P(REQ, HEAD))
    return jax.shard_map(
        on_device, mesh=fine, in_specs=in_specs, out_specs=out_specs, check_vma=False
    )
```

```python
import jax
import jax.numpy as jnp
from jax import lax
from jax.experimental import pallas as pl
from jax.experimental.pallas import tpu as pltpu
from jax.sharding import Mesh, PartitionSpec as P

HD = 128
PAGE = 64
MAXP = 8
GROUP = 8
ROWS = 4
QROWS = ROWS * GROUP
POOL = 32
CHIPS = 32
PEERS = 16
STATS = 8
SCALE = HD**-0.5
PLANE = ("y", "zq", "p")
SPARSE = ("y", "zq")
HEAD = ("zh", "x")
REQ = ("y", "zq", "p", "c")
BF = jnp.bfloat16
F32 = jnp.float32


def dot(a, b, ca, cb):
    return lax.dot_general(a, b, (((ca,), (cb,)), ((), ())), preferred_element_type=F32)


def own_kernel(pages_ref, len_ref, q_ref, new_ref, own_ref, acc_ref, top_ref, total_ref):
    tokens = POOL * PAGE
    scores = dot(q_ref[...], own_ref[0], 1, 1) * SCALE
    page_of = lax.broadcasted_iota(jnp.int32, (GROUP, tokens), 1) // PAGE
    weights, tops, totals, news = [], [], [], []
    for b in range(ROWS):
        count = jnp.zeros((GROUP, tokens), F32)
        for i in range(MAXP):
            page = jnp.where(i < len_ref[b], pages_ref[b, i], -1)
            count = count + jnp.where(page_of == page, 1.0, 0.0)
        s = jnp.where(count > 0.0, scores[b * GROUP : (b + 1) * GROUP], -jnp.inf)
        q = q_ref[b * GROUP : (b + 1) * GROUP].astype(F32)
        s_new = jnp.sum(q * new_ref[0, b : b + 1].astype(F32), axis=1, keepdims=True) * SCALE
        top = jnp.maximum(jnp.max(s, axis=1, keepdims=True), s_new)
        w = jnp.exp(s - top) * count
        w_new = jnp.exp(s_new - top)
        weights.append(w.astype(BF))
        tops.append(top)
        totals.append(jnp.sum(w, axis=1, keepdims=True) + w_new)
        news.append(w_new.astype(BF).astype(F32) * new_ref[1, b : b + 1].astype(F32))
    acc = dot(jnp.concatenate(weights, axis=0), own_ref[1], 1, 0)
    acc_ref[...] = acc + jnp.concatenate(news, axis=0)
    top_ref[...] = jnp.broadcast_to(jnp.concatenate(tops, axis=0), (QROWS, HD))
    total_ref[...] = jnp.broadcast_to(jnp.concatenate(totals, axis=0), (QROWS, HD))


def own_part(pages, own_len, q, new_kv, own_kv):
    smem = pl.BlockSpec(memory_space=pltpu.SMEM)
    vmem = pl.BlockSpec(memory_space=pltpu.VMEM)
    return pl.pallas_call(
        own_kernel,
        out_shape=[jax.ShapeDtypeStruct((QROWS, HD), F32)] * 3,
        in_specs=[smem, smem, vmem, vmem, vmem],
        out_specs=[vmem] * 3,
        compiler_params=pltpu.CompilerParams(vmem_limit_bytes=32 << 20),
        name="own_attention",
    )(pages, own_len, q, new_kv, own_kv)


def man_kernel(q_ref, kv_ref, out_ref):
    keys = jnp.concatenate([kv_ref[i, 0] for i in range(4)], axis=0)
    values = jnp.concatenate([kv_ref[i, 1] for i in range(4)], axis=0)
    row = lax.broadcasted_iota(jnp.int32, (STATS, HD), 0)
    for chunk in range(PEERS * QROWS // HD):
        s = dot(keys, q_ref[chunk * HD : (chunk + 1) * HD], 1, 1) * SCALE
        top = jnp.max(s, axis=0, keepdims=True).astype(BF).astype(F32)
        w = jnp.exp(s - top)
        total = jnp.sum(w, axis=0, keepdims=True)
        high = total.astype(BF).astype(F32)
        acc = dot(w.astype(BF), values, 0, 0).astype(BF)
        stats = jnp.where(row == 0, top, jnp.where(row == 1, high, jnp.where(row == 2, total - high, 0.0)))
        stats = stats.astype(BF)
        for j in range(HD // QROWS):
            to = chunk * (HD // QROWS) + j
            out_ref[to, 0:QROWS] = acc[j * QROWS : (j + 1) * QROWS]
            out_ref[to, QROWS : QROWS + STATS] = stats


def man_part(q_all, kv):
    vmem = pl.BlockSpec(memory_space=pltpu.VMEM)
    return pl.pallas_call(
        man_kernel,
        out_shape=jax.ShapeDtypeStruct((PEERS, QROWS + STATS, HD), BF),
        in_specs=[vmem, vmem],
        out_specs=vmem,
        compiler_params=pltpu.CompilerParams(vmem_limit_bytes=32 << 20),
        name="manifest_attention",
    )(q_all, kv)


def join_kernel(place_ref, parts_ref, acc_ref, top_ref, total_ref, out_ref, rows_ref):
    stats = parts_ref[:, QROWS : QROWS + STATS, :].reshape(PEERS * STATS, HD)
    lane = lax.broadcasted_iota(jnp.int32, (QROWS, HD), 1)
    row = lax.broadcasted_iota(jnp.int32, (QROWS, HD), 0)
    pick = jnp.where(lane == row + place_ref[0] * QROWS, 1.0, 0.0).astype(BF)
    s = dot(pick, stats, 1, 1)
    n = PEERS * STATS
    kind = lax.broadcasted_iota(jnp.int32, (QROWS, n), 1) % STATS
    totals = pltpu.roll(s, n - 1, 1) + pltpu.roll(s, n - 2, 1)
    own_top = top_ref[:, 0:1]
    top = jnp.maximum(jnp.max(jnp.where(kind == 0, s, -jnp.inf), axis=1, keepdims=True), own_top)
    factor = jnp.where(kind == 0, jnp.exp(jnp.minimum(s - top, 0.0)), 0.0)
    own_factor = jnp.exp(own_top - top)
    total = jnp.sum(factor * totals, axis=1, keepdims=True) + own_factor * total_ref[:, 0:1]
    acc = own_factor * acc_ref[...]
    for i in range(PEERS):
        acc = acc + factor[:, i * STATS : i * STATS + 1] * parts_ref[i, 0:QROWS].astype(F32)
    rows_ref[...] = acc / total
    for h in range(GROUP):
        rows = rows_ref[pl.ds(h, ROWS, stride=GROUP), :].astype(BF)
        for i in range(CHIPS):
            out_ref[i, :, h * HD : (h + 1) * HD] = rows


def join_part(place, parts, acc, top, total):
    smem = pl.BlockSpec(memory_space=pltpu.SMEM)
    vmem = pl.BlockSpec(memory_space=pltpu.VMEM)
    return pl.pallas_call(
        join_kernel,
        out_shape=jax.ShapeDtypeStruct((CHIPS, ROWS, GROUP * HD), BF),
        in_specs=[smem, vmem, vmem, vmem, vmem],
        out_specs=vmem,
        scratch_shapes=[pltpu.VMEM((QROWS, HD), F32)],
        compiler_params=pltpu.CompilerParams(vmem_limit_bytes=32 << 20),
        name="join_attention",
    )(place, parts, acc, top, total)


def project_kernel(x_ref, w0_ref, w1_ref, out_ref):
    w = jnp.concatenate([w0_ref[...], w1_ref[...]], axis=1)
    out_ref[...] = dot(x_ref[...], w, 1, 0).astype(BF)


def add_kernel(a_ref, out_ref):
    block = (a_ref[0].astype(F32) + a_ref[1].astype(F32)).astype(BF)
    for i in range(4):
        out_ref[i] = block


def mlp_kernel(x_ref, g0_ref, g1_ref, u0_ref, u1_ref, out_ref):
    x = x_ref[...]
    turned = x.astype(F32).reshape(CHIPS // 2, 2 * ROWS, 2 * HD)
    turned = jnp.concatenate([turned[:, ROWS:], turned[:, :ROWS]], axis=1).reshape(CHIPS * ROWS, 2 * HD).astype(BF)
    gate = dot(x, jnp.concatenate([g0_ref[...], g1_ref[...]], axis=0), 1, 0)
    up = dot(turned, jnp.concatenate([u0_ref[...], u1_ref[...]], axis=0), 1, 0)
    low = lax.broadcasted_iota(jnp.int32, (2 * ROWS, gate.shape[1]), 0) < ROWS
    for j in range(CHIPS // 2):
        at = slice(2 * j * ROWS, 2 * (j + 1) * ROWS)
        out_ref[2 * j] = jnp.where(low, gate[at], up[at]).astype(BF)
        out_ref[2 * j + 1] = jnp.where(low, up[at], gate[at]).astype(BF)


def dense(kernel, name, out_shape, *args):
    vmem = pl.BlockSpec(memory_space=pltpu.VMEM)
    return pl.pallas_call(
        kernel,
        out_shape=jax.ShapeDtypeStruct(out_shape, BF),
        in_specs=[vmem] * len(args),
        out_specs=vmem,
        compiler_params=pltpu.CompilerParams(vmem_limit_bytes=40 << 20),
        name=name,
    )(*args)


def swap(x):
    return lax.ppermute(x, "c", [(0, 1), (1, 0)])


def exchange(x, axes):
    return lax.all_to_all(x, axes, 0, 0, tiled=True)


def on_device(queries, new_kv, own_kv, man_kv, pages, own_len, resid, w_out, w_gate, w_up):
    core = lax.axis_index("c")
    tie = lax.optimization_barrier
    width = w_gate.shape[1]
    rows = CHIPS * ROWS
    q = queries.reshape(QROWS, HD)
    q_all = exchange(jnp.broadcast_to(q[None], (PEERS, QROWS, HD)), SPARSE).reshape(PEERS * QROWS, HD)
    kv = lax.all_gather(man_kv.reshape(1, 2, 2 * PAGE, HD), ("p", "c"), axis=0, tiled=True)
    parts = exchange(man_part(q_all, kv), SPARSE)
    own = own_part(pages, own_len, q, new_kv, own_kv.reshape(2, POOL * PAGE, HD))
    parts, own, w_out_c = tie((parts, own, swap(w_out)))
    place = (lax.axis_index(SPARSE) % 4).astype(jnp.int32).reshape(1)
    attn = exchange(join_part(place, parts, *own), PLANE).reshape(rows, GROUP * HD)
    attn, w_gate_c, w_up_c = tie((attn, swap(w_gate), swap(w_up)))

    share = dense(project_kernel, "project", (rows, 2 * HD), attn, w_out, w_out_c)
    shares = lax.all_gather(share, "zh", axis=0)
    shares, resid = tie((shares, resid))
    heads = exchange(dense(add_kernel, "add_shares", (4, rows, 2 * HD), shares), "x")
    res = resid.reshape(CHIPS, 2, ROWS, HD)
    mine = jnp.where(core == 0, res[:, 0], res[:, 1])
    theirs = swap(jnp.where(core == 0, res[:, 1], res[:, 0]))
    res = jnp.concatenate([mine, theirs], axis=-1).reshape(rows, 2 * HD).astype(F32)
    out2 = (res + heads.astype(F32).sum(0)).astype(BF)
    both = dense(mlp_kernel, "gate_up", (CHIPS, 2 * ROWS, width), out2, w_gate, w_gate_c, w_up, w_up_c)
    joined = exchange(both, PLANE).astype(F32).sum(0)
    odd = lax.axis_index("p") == 1
    gate = jnp.where(odd, joined[ROWS:], joined[:ROWS])
    up = jnp.where(odd, joined[:ROWS], joined[ROWS:])
    hidden = (jax.nn.silu(gate) * up).astype(BF)

    kept = out2[:, :HD].reshape(CHIPS, 1, ROWS, HD)
    given = swap(out2[:, HD:]).reshape(CHIPS, 1, ROWS, HD)
    first = jnp.where(core == 0, kept, given)
    second = jnp.where(core == 0, given, kept)
    resid_out = jnp.concatenate([first, second], axis=1).reshape(CHIPS * 2 * ROWS, HD)
    return (resid_out, hidden)


def solution(mesh):
    fine = Mesh(mesh.devices.reshape(8, 2, 2, 2, 2, 4), ("y", "zq", "p", "c", "zh", "x"))
    in_specs = (
        P(REQ, HEAD),
        P(None, REQ, HEAD),
        P(None, REQ, None, HEAD),
        P(None, REQ, None, HEAD),
        P(REQ, None),
        P(REQ),
        P(None, REQ),
        P(HEAD, REQ),
        P(REQ, HEAD),
        P(REQ, HEAD),
    )
    out_specs = (P(None, REQ), P(REQ, HEAD))
    return jax.shard_map(
        on_device, mesh=fine, in_specs=in_specs, out_specs=out_specs, check_vma=False
    )
```

```python
import jax
import jax.numpy as jnp
from jax import lax
from jax.experimental import pallas as pl
from jax.experimental.pallas import tpu as pltpu
from jax.sharding import Mesh, PartitionSpec as P

HD = 128
PAGE = 64
MAXP = 8
GROUP = 8
ROWS = 4
QROWS = ROWS * GROUP
POOL = 32
CHIPS = 32
PEERS = 16
STATS = 8
SCALE = HD**-0.5
PLANE = ("y", "zq", "p")
SPARSE = ("y", "zq")
HEAD = ("zh", "x")
REQ = ("y", "zq", "p", "c")
BF = jnp.bfloat16
F32 = jnp.float32


def dot(a, b, ca, cb):
    return lax.dot_general(a, b, (((ca,), (cb,)), ((), ())), preferred_element_type=F32)


def own_kernel(pages_ref, len_ref, q_ref, new_ref, own_ref, acc_ref, top_ref, total_ref):
    tokens = POOL * PAGE
    scores = dot(q_ref[...], own_ref[0], 1, 1) * SCALE
    page_of = lax.broadcasted_iota(jnp.int32, (GROUP, tokens), 1) // PAGE
    weights, tops, totals, news = [], [], [], []
    for b in range(ROWS):
        count = jnp.zeros((GROUP, tokens), F32)
        for i in range(MAXP):
            page = jnp.where(i < len_ref[b], pages_ref[b, i], -1)
            count = count + jnp.where(page_of == page, 1.0, 0.0)
        s = jnp.where(count > 0.0, scores[b * GROUP : (b + 1) * GROUP], -jnp.inf)
        q = q_ref[b * GROUP : (b + 1) * GROUP].astype(F32)
        s_new = jnp.sum(q * new_ref[0, b : b + 1].astype(F32), axis=1, keepdims=True) * SCALE
        top = jnp.maximum(jnp.max(s, axis=1, keepdims=True), s_new)
        w = jnp.exp(s - top) * count
        w_new = jnp.exp(s_new - top)
        weights.append(w.astype(BF))
        tops.append(top)
        totals.append(jnp.sum(w, axis=1, keepdims=True) + w_new)
        news.append(w_new.astype(BF).astype(F32) * new_ref[1, b : b + 1].astype(F32))
    acc = dot(jnp.concatenate(weights, axis=0), own_ref[1], 1, 0)
    acc_ref[...] = acc + jnp.concatenate(news, axis=0)
    top_ref[...] = jnp.broadcast_to(jnp.concatenate(tops, axis=0), (QROWS, HD))
    total_ref[...] = jnp.broadcast_to(jnp.concatenate(totals, axis=0), (QROWS, HD))


def own_part(pages, own_len, q, new_kv, own_kv):
    smem = pl.BlockSpec(memory_space=pltpu.SMEM)
    vmem = pl.BlockSpec(memory_space=pltpu.VMEM)
    return pl.pallas_call(
        own_kernel,
        out_shape=[jax.ShapeDtypeStruct((QROWS, HD), F32)] * 3,
        in_specs=[smem, smem, vmem, vmem, vmem],
        out_specs=[vmem] * 3,
        compiler_params=pltpu.CompilerParams(vmem_limit_bytes=32 << 20),
        name="own_attention",
    )(pages, own_len, q, new_kv, own_kv)


def man_kernel(q_ref, kv_ref, out_ref):
    keys = jnp.concatenate([kv_ref[i, 0] for i in range(4)], axis=0)
    values = jnp.concatenate([kv_ref[i, 1] for i in range(4)], axis=0)
    row = lax.broadcasted_iota(jnp.int32, (STATS, HD), 0)
    for chunk in range(PEERS * QROWS // HD):
        s = dot(keys, q_ref[chunk * HD : (chunk + 1) * HD], 1, 1) * SCALE
        top = jnp.max(s, axis=0, keepdims=True).astype(BF).astype(F32)
        w = jnp.exp(s - top)
        total = jnp.sum(w, axis=0, keepdims=True)
        high = total.astype(BF).astype(F32)
        acc = dot(w.astype(BF), values, 0, 0).astype(BF)
        stats = jnp.where(row == 0, top, jnp.where(row == 1, high, jnp.where(row == 2, total - high, 0.0)))
        stats = stats.astype(BF)
        for j in range(HD // QROWS):
            to = chunk * (HD // QROWS) + j
            out_ref[to, 0:QROWS] = acc[j * QROWS : (j + 1) * QROWS]
            out_ref[to, QROWS : QROWS + STATS] = stats


def man_part(q_all, kv):
    vmem = pl.BlockSpec(memory_space=pltpu.VMEM)
    return pl.pallas_call(
        man_kernel,
        out_shape=jax.ShapeDtypeStruct((PEERS, QROWS + STATS, HD), BF),
        in_specs=[vmem, vmem],
        out_specs=vmem,
        compiler_params=pltpu.CompilerParams(vmem_limit_bytes=32 << 20),
        name="manifest_attention",
    )(q_all, kv)


def join_kernel(place_ref, parts_ref, acc_ref, top_ref, total_ref, out_ref, rows_ref):
    stats = parts_ref[:, QROWS : QROWS + STATS, :].reshape(PEERS * STATS, HD)
    lane = lax.broadcasted_iota(jnp.int32, (QROWS, HD), 1)
    row = lax.broadcasted_iota(jnp.int32, (QROWS, HD), 0)
    pick = jnp.where(lane == row + place_ref[0] * QROWS, 1.0, 0.0).astype(BF)
    s = dot(pick, stats, 1, 1)
    n = PEERS * STATS
    kind = lax.broadcasted_iota(jnp.int32, (QROWS, n), 1) % STATS
    totals = pltpu.roll(s, n - 1, 1) + pltpu.roll(s, n - 2, 1)
    own_top = top_ref[:, 0:1]
    top = jnp.maximum(jnp.max(jnp.where(kind == 0, s, -jnp.inf), axis=1, keepdims=True), own_top)
    factor = jnp.where(kind == 0, jnp.exp(jnp.minimum(s - top, 0.0)), 0.0)
    own_factor = jnp.exp(own_top - top)
    total = jnp.sum(factor * totals, axis=1, keepdims=True) + own_factor * total_ref[:, 0:1]
    acc = own_factor * acc_ref[...]
    for i in range(PEERS):
        acc = acc + factor[:, i * STATS : i * STATS + 1] * parts_ref[i, 0:QROWS].astype(F32)
    rows_ref[...] = acc / total
    for h in range(GROUP):
        rows = rows_ref[pl.ds(h, ROWS, stride=GROUP), :].astype(BF)
        for i in range(CHIPS):
            out_ref[i, :, h * HD : (h + 1) * HD] = rows


def join_part(place, parts, acc, top, total):
    smem = pl.BlockSpec(memory_space=pltpu.SMEM)
    vmem = pl.BlockSpec(memory_space=pltpu.VMEM)
    return pl.pallas_call(
        join_kernel,
        out_shape=jax.ShapeDtypeStruct((CHIPS, ROWS, GROUP * HD), BF),
        in_specs=[smem, vmem, vmem, vmem, vmem],
        out_specs=vmem,
        scratch_shapes=[pltpu.VMEM((QROWS, HD), F32)],
        compiler_params=pltpu.CompilerParams(vmem_limit_bytes=32 << 20),
        name="join_attention",
    )(place, parts, acc, top, total)


def project_kernel(x_ref, w0_ref, w1_ref, out_ref):
    w = jnp.concatenate([w0_ref[...], w1_ref[...]], axis=1)
    out_ref[...] = dot(x_ref[...], w, 1, 0).astype(BF)


def add_kernel(a_ref, out_ref):
    block = (a_ref[0].astype(F32) + a_ref[1].astype(F32)).astype(BF)
    for i in range(4):
        out_ref[i] = block


def mlp_kernel(side_ref, x_ref, both_ref, w0_ref, w1_ref, w2_ref, w3_ref, out_ref):
    def turn(x):
        x = x.astype(F32).reshape(CHIPS // 2, 2 * ROWS, 2 * HD)
        return jnp.concatenate([x[:, ROWS:], x[:, :ROWS]], axis=1).reshape(CHIPS * ROWS, 2 * HD).astype(BF)

    x, other = x_ref[...], both_ref[1 - side_ref[0]]
    half = w0_ref.shape[1] // 2

    def product(a, b, at):
        w = [w_ref[:, at] for w_ref in (w0_ref, w1_ref, w2_ref, w3_ref)]
        return dot(a, jnp.concatenate(w[:2], axis=0), 1, 0) + dot(b, jnp.concatenate(w[2:], axis=0), 1, 0)

    left = product(x, other, slice(0, half))
    right = product(turn(x), turn(other), slice(half, 2 * half))
    low = lax.broadcasted_iota(jnp.int32, (2 * ROWS, half), 0) < ROWS
    for j in range(CHIPS // 2):
        at = slice(2 * j * ROWS, 2 * (j + 1) * ROWS)
        out_ref[2 * j] = jnp.where(low, left[at], right[at]).astype(BF)
        out_ref[2 * j + 1] = jnp.where(low, right[at], left[at]).astype(BF)


def dense(kernel, name, out_shape, *args, scalars=0):
    vmem = pl.BlockSpec(memory_space=pltpu.VMEM)
    smem = pl.BlockSpec(memory_space=pltpu.SMEM)
    return pl.pallas_call(
        kernel,
        out_shape=jax.ShapeDtypeStruct(out_shape, BF),
        in_specs=[smem] * scalars + [vmem] * (len(args) - scalars),
        out_specs=vmem,
        compiler_params=pltpu.CompilerParams(vmem_limit_bytes=40 << 20),
        name=name,
    )(*args)


def swap(x):
    return lax.ppermute(x, "c", [(0, 1), (1, 0)])


def pair(x):
    return lax.ppermute(x, "p", [(0, 1), (1, 0)])


def exchange(x, axes):
    return lax.all_to_all(x, axes, 0, 0, tiled=True)


def on_device(queries, new_kv, own_kv, man_kv, pages, own_len, resid, w_out, w_gate, w_up):
    core = lax.axis_index("c")
    tie = lax.optimization_barrier
    width = w_gate.shape[1]
    rows = CHIPS * ROWS
    q = queries.reshape(QROWS, HD)
    q_all = exchange(jnp.broadcast_to(q[None], (PEERS, QROWS, HD)), SPARSE).reshape(PEERS * QROWS, HD)
    kv = lax.all_gather(man_kv.reshape(1, 2, 2 * PAGE, HD), ("p", "c"), axis=0, tiled=True)
    parts = exchange(man_part(q_all, kv), SPARSE)
    own = own_part(pages, own_len, q, new_kv, own_kv.reshape(2, POOL * PAGE, HD))
    parts, own, w_out_c = tie((parts, own, swap(w_out)))
    place = (lax.axis_index(SPARSE) % 4).astype(jnp.int32).reshape(1)
    attn = exchange(join_part(place, parts, *own), PLANE).reshape(rows, GROUP * HD)
    side = lax.axis_index("p")
    w_keep = jnp.where(side == 0, w_gate, w_up)
    w_pair = pair(jnp.where(side == 0, w_up, w_gate))
    attn, w_keep_c = tie((attn, swap(w_keep)))

    share = dense(project_kernel, "project", (rows, 2 * HD), attn, w_out, w_out_c)
    shares = lax.all_gather(share, "zh", axis=0)
    shares, resid, w_pair = tie((shares, resid, w_pair))
    heads = exchange(dense(add_kernel, "add_shares", (4, rows, 2 * HD), shares), "x")
    res = resid.reshape(CHIPS, 2, ROWS, HD)
    mine = jnp.where(core == 0, res[:, 0], res[:, 1])
    theirs = swap(jnp.where(core == 0, res[:, 1], res[:, 0]))
    res = jnp.concatenate([mine, theirs], axis=-1).reshape(rows, 2 * HD).astype(F32)
    out2 = (res + heads.astype(F32).sum(0)).astype(BF)
    place = side.astype(jnp.int32).reshape(1)
    pairs = lax.all_gather(out2, "p", axis=0)
    both = dense(
        mlp_kernel, "gate_up", (CHIPS, 2 * ROWS, width // 2),
        place, out2, pairs, w_keep, w_keep_c, w_pair, swap(w_pair), scalars=1,
    )
    joined = exchange(both, PLANE).reshape(PEERS, 2, 2 * ROWS, width // 2).astype(F32).sum(0)
    first, second = joined[:, :ROWS], joined[:, ROWS:]
    odd = side == 1
    joined = jnp.concatenate([jnp.where(odd, second, first), jnp.where(odd, first, second)], axis=-1)
    hidden = (jax.nn.silu(joined[0]) * joined[1]).astype(BF)

    kept = out2[:, :HD].reshape(CHIPS, 1, ROWS, HD)
    given = swap(out2[:, HD:]).reshape(CHIPS, 1, ROWS, HD)
    first = jnp.where(core == 0, kept, given)
    second = jnp.where(core == 0, given, kept)
    resid_out = jnp.concatenate([first, second], axis=1).reshape(CHIPS * 2 * ROWS, HD)
    return (resid_out, hidden)


def solution(mesh):
    fine = Mesh(mesh.devices.reshape(8, 2, 2, 2, 2, 4), ("y", "zq", "p", "c", "zh", "x"))
    in_specs = (
        P(REQ, HEAD),
        P(None, REQ, HEAD),
        P(None, REQ, None, HEAD),
        P(None, REQ, None, HEAD),
        P(REQ, None),
        P(REQ),
        P(None, REQ),
        P(HEAD, REQ),
        P(REQ, HEAD),
        P(REQ, HEAD),
    )
    out_specs = (P(None, REQ), P(REQ, HEAD))
    return jax.shard_map(
        on_device, mesh=fine, in_specs=in_specs, out_specs=out_specs, check_vma=False
    )
```

```python
import jax
import jax.numpy as jnp
from jax import lax
from jax.experimental import pallas as pl
from jax.experimental.pallas import tpu as pltpu
from jax.sharding import Mesh, PartitionSpec as P

HD = 128
PAGE = 64
MAXP = 8
GROUP = 8
ROWS = 4
QROWS = ROWS * GROUP
POOL = 32
CHIPS = 32
PEERS = 16
STATS = 8
SCALE = HD**-0.5
PLANE = ("y", "zq", "p")
SPARSE = ("y", "zq")
HEAD = ("zh", "x")
REQ = ("y", "zq", "p", "c")
BF = jnp.bfloat16
F32 = jnp.float32


def dot(a, b, ca, cb):
    return lax.dot_general(a, b, (((ca,), (cb,)), ((), ())), preferred_element_type=F32)


def own_kernel(pages_ref, len_ref, q_ref, new_ref, own_ref, acc_ref, top_ref, total_ref):
    tokens = POOL * PAGE
    scores = dot(q_ref[...], own_ref[0], 1, 1) * SCALE
    page_of = lax.broadcasted_iota(jnp.int32, (GROUP, tokens), 1) // PAGE
    weights, tops, totals, news = [], [], [], []
    for b in range(ROWS):
        count = jnp.zeros((GROUP, tokens), F32)
        for i in range(MAXP):
            page = jnp.where(i < len_ref[b], pages_ref[b, i], -1)
            count = count + jnp.where(page_of == page, 1.0, 0.0)
        s = jnp.where(count > 0.0, scores[b * GROUP : (b + 1) * GROUP], -jnp.inf)
        q = q_ref[b * GROUP : (b + 1) * GROUP].astype(F32)
        s_new = jnp.sum(q * new_ref[0, b : b + 1].astype(F32), axis=1, keepdims=True) * SCALE
        top = jnp.maximum(jnp.max(s, axis=1, keepdims=True), s_new)
        w = jnp.exp(s - top) * count
        w_new = jnp.exp(s_new - top)
        weights.append(w.astype(BF))
        tops.append(top)
        totals.append(jnp.sum(w, axis=1, keepdims=True) + w_new)
        news.append(w_new.astype(BF).astype(F32) * new_ref[1, b : b + 1].astype(F32))
    acc = dot(jnp.concatenate(weights, axis=0), own_ref[1], 1, 0)
    acc_ref[...] = acc + jnp.concatenate(news, axis=0)
    top_ref[...] = jnp.broadcast_to(jnp.concatenate(tops, axis=0), (QROWS, HD))
    total_ref[...] = jnp.broadcast_to(jnp.concatenate(totals, axis=0), (QROWS, HD))


def own_part(pages, own_len, q, new_kv, own_kv):
    smem = pl.BlockSpec(memory_space=pltpu.SMEM)
    vmem = pl.BlockSpec(memory_space=pltpu.VMEM)
    return pl.pallas_call(
        own_kernel,
        out_shape=[jax.ShapeDtypeStruct((QROWS, HD), F32)] * 3,
        in_specs=[smem, smem, vmem, vmem, vmem],
        out_specs=[vmem] * 3,
        compiler_params=pltpu.CompilerParams(vmem_limit_bytes=32 << 20),
        name="own_attention",
    )(pages, own_len, q, new_kv, own_kv)


def man_kernel(q_ref, kv_ref, out_ref):
    keys = jnp.concatenate([kv_ref[i, 0] for i in range(4)], axis=0)
    values = jnp.concatenate([kv_ref[i, 1] for i in range(4)], axis=0)
    row = lax.broadcasted_iota(jnp.int32, (STATS, HD), 0)
    for chunk in range(PEERS * QROWS // HD):
        s = dot(keys, q_ref[chunk * HD : (chunk + 1) * HD], 1, 1) * SCALE
        top = jnp.max(s, axis=0, keepdims=True).astype(BF).astype(F32)
        w = jnp.exp(s - top)
        total = jnp.sum(w, axis=0, keepdims=True)
        high = total.astype(BF).astype(F32)
        acc = dot(w.astype(BF), values, 0, 0).astype(BF)
        stats = jnp.where(row == 0, top, jnp.where(row == 1, high, jnp.where(row == 2, total - high, 0.0)))
        stats = stats.astype(BF)
        for j in range(HD // QROWS):
            to = chunk * (HD // QROWS) + j
            out_ref[to, 0:QROWS] = acc[j * QROWS : (j + 1) * QROWS]
            out_ref[to, QROWS : QROWS + STATS] = stats


def man_part(q_all, kv):
    vmem = pl.BlockSpec(memory_space=pltpu.VMEM)
    return pl.pallas_call(
        man_kernel,
        out_shape=jax.ShapeDtypeStruct((PEERS, QROWS + STATS, HD), BF),
        in_specs=[vmem, vmem],
        out_specs=vmem,
        compiler_params=pltpu.CompilerParams(vmem_limit_bytes=32 << 20),
        name="manifest_attention",
    )(q_all, kv)


def join_kernel(place_ref, parts_ref, acc_ref, top_ref, total_ref, out_ref, rows_ref):
    stats = parts_ref[:, QROWS : QROWS + STATS, :].reshape(PEERS * STATS, HD)
    lane = lax.broadcasted_iota(jnp.int32, (QROWS, HD), 1)
    row = lax.broadcasted_iota(jnp.int32, (QROWS, HD), 0)
    pick = jnp.where(lane == row + place_ref[0] * QROWS, 1.0, 0.0).astype(BF)
    s = dot(pick, stats, 1, 1)
    n = PEERS * STATS
    kind = lax.broadcasted_iota(jnp.int32, (QROWS, n), 1) % STATS
    totals = pltpu.roll(s, n - 1, 1) + pltpu.roll(s, n - 2, 1)
    own_top = top_ref[:, 0:1]
    top = jnp.maximum(jnp.max(jnp.where(kind == 0, s, -jnp.inf), axis=1, keepdims=True), own_top)
    factor = jnp.where(kind == 0, jnp.exp(jnp.minimum(s - top, 0.0)), 0.0)
    own_factor = jnp.exp(own_top - top)
    total = jnp.sum(factor * totals, axis=1, keepdims=True) + own_factor * total_ref[:, 0:1]
    acc = own_factor * acc_ref[...]
    for i in range(PEERS):
        acc = acc + factor[:, i * STATS : i * STATS + 1] * parts_ref[i, 0:QROWS].astype(F32)
    rows_ref[...] = acc / total
    for h in range(GROUP):
        rows = rows_ref[pl.ds(h, ROWS, stride=GROUP), :].astype(BF)
        for i in range(CHIPS):
            out_ref[i, :, h * HD : (h + 1) * HD] = rows


def join_part(place, parts, acc, top, total):
    smem = pl.BlockSpec(memory_space=pltpu.SMEM)
    vmem = pl.BlockSpec(memory_space=pltpu.VMEM)
    return pl.pallas_call(
        join_kernel,
        out_shape=jax.ShapeDtypeStruct((CHIPS, ROWS, GROUP * HD), BF),
        in_specs=[smem, vmem, vmem, vmem, vmem],
        out_specs=vmem,
        scratch_shapes=[pltpu.VMEM((QROWS, HD), F32)],
        compiler_params=pltpu.CompilerParams(vmem_limit_bytes=32 << 20),
        name="join_attention",
    )(place, parts, acc, top, total)


def project_kernel(x_ref, w0_ref, w1_ref, out_ref):
    w = jnp.concatenate([w0_ref[...], w1_ref[...]], axis=1)
    out_ref[...] = dot(x_ref[...], w, 1, 0).astype(BF)


def add_kernel(a_ref, out_ref):
    block = (a_ref[0].astype(F32) + a_ref[1].astype(F32)).astype(BF)
    for i in range(4):
        out_ref[i] = block


def mlp_kernel(side_ref, x_ref, both_ref, w0_ref, w1_ref, w2_ref, w3_ref, out_ref):
    def turn(x):
        x = x.astype(F32).reshape(CHIPS // 2, 2 * ROWS, 2 * HD)
        return jnp.concatenate([x[:, ROWS:], x[:, :ROWS]], axis=1).reshape(CHIPS * ROWS, 2 * HD).astype(BF)

    x, other = x_ref[...], both_ref[1 - side_ref[0]]
    half = w0_ref.shape[1] // 2

    def product(a, b, at):
        w = [w_ref[:, at] for w_ref in (w0_ref, w1_ref, w2_ref, w3_ref)]
        return dot(a, jnp.concatenate(w[:2], axis=0), 1, 0) + dot(b, jnp.concatenate(w[2:], axis=0), 1, 0)

    left = product(x, other, slice(0, half))
    right = product(turn(x), turn(other), slice(half, 2 * half))
    low = lax.broadcasted_iota(jnp.int32, (2 * ROWS, half), 0) < ROWS
    for j in range(CHIPS // 2):
        at = slice(2 * j * ROWS, 2 * (j + 1) * ROWS)
        out_ref[2 * j] = jnp.where(low, left[at], right[at]).astype(BF)
        out_ref[2 * j + 1] = jnp.where(low, right[at], left[at]).astype(BF)


def dense(kernel, name, out_shape, *args, scalars=0):
    vmem = pl.BlockSpec(memory_space=pltpu.VMEM)
    smem = pl.BlockSpec(memory_space=pltpu.SMEM)
    return pl.pallas_call(
        kernel,
        out_shape=jax.ShapeDtypeStruct(out_shape, BF),
        in_specs=[smem] * scalars + [vmem] * (len(args) - scalars),
        out_specs=vmem,
        compiler_params=pltpu.CompilerParams(vmem_limit_bytes=40 << 20),
        name=name,
    )(*args)


def swap(x):
    return lax.ppermute(x, "c", [(0, 1), (1, 0)])


def pair(x):
    return lax.ppermute(x, "p", [(0, 1), (1, 0)])


def exchange(x, axes):
    return lax.all_to_all(x, axes, 0, 0, tiled=True)


def on_device(queries, new_kv, own_kv, man_kv, pages, own_len, resid, w_out, w_gate, w_up):
    core = lax.axis_index("c")
    tie = lax.optimization_barrier
    width = w_gate.shape[1]
    rows = CHIPS * ROWS
    q = queries.reshape(QROWS, HD)
    q_all = exchange(jnp.broadcast_to(q[None], (PEERS, QROWS, HD)), SPARSE).reshape(PEERS * QROWS, HD)
    kv = lax.all_gather(man_kv.reshape(1, 2, 2 * PAGE, HD), ("p", "c"), axis=0, tiled=True)
    parts = exchange(man_part(q_all, kv), SPARSE)
    own = own_part(pages, own_len, q, new_kv, own_kv.reshape(2, POOL * PAGE, HD))
    side = lax.axis_index("p")
    w_keep = jnp.where(side == 0, w_gate, w_up)
    w_send = jnp.where(side == 0, w_up, w_gate)
    w_pair = [pair(w_send[: HD // 2]), pair(w_send[HD // 2 :])]
    parts, own, w_out_c, w_pair[0] = tie((parts, own, swap(w_out), w_pair[0]))
    w_pair = jnp.concatenate(w_pair, axis=0)
    place = (lax.axis_index(SPARSE) % 4).astype(jnp.int32).reshape(1)
    attn = exchange(join_part(place, parts, *own), PLANE).reshape(rows, GROUP * HD)
    attn, w_keep_c, w_pair = tie((attn, swap(w_keep), w_pair))

    share = dense(project_kernel, "project", (rows, 2 * HD), attn, w_out, w_out_c)
    shares = lax.all_gather(share, "zh", axis=0)
    shares, resid = tie((shares, resid))
    heads = exchange(dense(add_kernel, "add_shares", (4, rows, 2 * HD), shares), "x")
    res = resid.reshape(CHIPS, 2, ROWS, HD)
    mine = jnp.where(core == 0, res[:, 0], res[:, 1])
    theirs = swap(jnp.where(core == 0, res[:, 1], res[:, 0]))
    res = jnp.concatenate([mine, theirs], axis=-1).reshape(rows, 2 * HD).astype(F32)
    out2 = (res + heads.astype(F32).sum(0)).astype(BF)
    place = side.astype(jnp.int32).reshape(1)
    pairs = lax.all_gather(out2, "p", axis=0)
    both = dense(
        mlp_kernel, "gate_up", (CHIPS, 2 * ROWS, width // 2),
        place, out2, pairs, w_keep, w_keep_c, w_pair, swap(w_pair), scalars=1,
    )
    joined = exchange(both, PLANE).reshape(PEERS, 2, 2 * ROWS, width // 2).astype(F32).sum(0)
    first, second = joined[:, :ROWS], joined[:, ROWS:]
    odd = side == 1
    joined = jnp.concatenate([jnp.where(odd, second, first), jnp.where(odd, first, second)], axis=-1)
    hidden = (jax.nn.silu(joined[0]) * joined[1]).astype(BF)

    kept = out2[:, :HD].reshape(CHIPS, 1, ROWS, HD)
    given = swap(out2[:, HD:]).reshape(CHIPS, 1, ROWS, HD)
    first = jnp.where(core == 0, kept, given)
    second = jnp.where(core == 0, given, kept)
    resid_out = jnp.concatenate([first, second], axis=1).reshape(CHIPS * 2 * ROWS, HD)
    return (resid_out, hidden)


def solution(mesh):
    fine = Mesh(mesh.devices.reshape(8, 2, 2, 2, 2, 4), ("y", "zq", "p", "c", "zh", "x"))
    in_specs = (
        P(REQ, HEAD),
        P(None, REQ, HEAD),
        P(None, REQ, None, HEAD),
        P(None, REQ, None, HEAD),
        P(REQ, None),
        P(REQ),
        P(None, REQ),
        P(HEAD, REQ),
        P(REQ, HEAD),
        P(REQ, HEAD),
    )
    out_specs = (P(None, REQ), P(REQ, HEAD))
    return jax.shard_map(
        on_device, mesh=fine, in_specs=in_specs, out_specs=out_specs, check_vma=False
    )
```

```python
import jax
import jax.numpy as jnp
from jax import lax
from jax.experimental import pallas as pl
from jax.experimental.pallas import tpu as pltpu
from jax.sharding import Mesh, PartitionSpec as P

HD = 128
PAGE = 64
MAXP = 8
GROUP = 8
ROWS = 4
QROWS = ROWS * GROUP
POOL = 32
CHIPS = 32
PEERS = 16
STATS = 8
SCALE = HD**-0.5
PLANE = ("y", "p", "zq")
SPARSE = ("y", "zq")
HEAD = ("zh", "x")
REQ = ("y", "p", "zq", "c")
BF = jnp.bfloat16
F32 = jnp.float32


def dot(a, b, ca, cb):
    return lax.dot_general(a, b, (((ca,), (cb,)), ((), ())), preferred_element_type=F32)


def own_kernel(pages_ref, len_ref, q_ref, new_ref, own_ref, acc_ref, top_ref, total_ref):
    tokens = POOL * PAGE
    scores = dot(q_ref[...], own_ref[0], 1, 1) * SCALE
    page_of = lax.broadcasted_iota(jnp.int32, (GROUP, tokens), 1) // PAGE
    weights, tops, totals, news = [], [], [], []
    for b in range(ROWS):
        count = jnp.zeros((GROUP, tokens), F32)
        for i in range(MAXP):
            page = jnp.where(i < len_ref[b], pages_ref[b, i], -1)
            count = count + jnp.where(page_of == page, 1.0, 0.0)
        s = jnp.where(count > 0.0, scores[b * GROUP : (b + 1) * GROUP], -jnp.inf)
        q = q_ref[b * GROUP : (b + 1) * GROUP].astype(F32)
        s_new = jnp.sum(q * new_ref[0, b : b + 1].astype(F32), axis=1, keepdims=True) * SCALE
        top = jnp.maximum(jnp.max(s, axis=1, keepdims=True), s_new)
        w = jnp.exp(s - top) * count
        w_new = jnp.exp(s_new - top)
        weights.append(w.astype(BF))
        tops.append(top)
        totals.append(jnp.sum(w, axis=1, keepdims=True) + w_new)
        news.append(w_new.astype(BF).astype(F32) * new_ref[1, b : b + 1].astype(F32))
    acc = dot(jnp.concatenate(weights, axis=0), own_ref[1], 1, 0)
    acc_ref[...] = acc + jnp.concatenate(news, axis=0)
    top_ref[...] = jnp.broadcast_to(jnp.concatenate(tops, axis=0), (QROWS, HD))
    total_ref[...] = jnp.broadcast_to(jnp.concatenate(totals, axis=0), (QROWS, HD))


def own_part(pages, own_len, q, new_kv, own_kv):
    smem = pl.BlockSpec(memory_space=pltpu.SMEM)
    vmem = pl.BlockSpec(memory_space=pltpu.VMEM)
    return pl.pallas_call(
        own_kernel,
        out_shape=[jax.ShapeDtypeStruct((QROWS, HD), F32)] * 3,
        in_specs=[smem, smem, vmem, vmem, vmem],
        out_specs=[vmem] * 3,
        compiler_params=pltpu.CompilerParams(vmem_limit_bytes=32 << 20),
        name="own_attention",
    )(pages, own_len, q, new_kv, own_kv)


def man_kernel(q_ref, kv_ref, out_ref):
    keys = jnp.concatenate([kv_ref[i, 0] for i in range(4)], axis=0)
    values = jnp.concatenate([kv_ref[i, 1] for i in range(4)], axis=0)
    row = lax.broadcasted_iota(jnp.int32, (STATS, HD), 0)
    for chunk in range(PEERS * QROWS // HD):
        s = dot(keys, q_ref[chunk * HD : (chunk + 1) * HD], 1, 1) * SCALE
        top = jnp.max(s, axis=0, keepdims=True).astype(BF).astype(F32)
        w = jnp.exp(s - top)
        total = jnp.sum(w, axis=0, keepdims=True)
        high = total.astype(BF).astype(F32)
        acc = dot(w.astype(BF), values, 0, 0).astype(BF)
        stats = jnp.where(row == 0, top, jnp.where(row == 1, high, jnp.where(row == 2, total - high, 0.0)))
        stats = stats.astype(BF)
        for j in range(HD // QROWS):
            to = chunk * (HD // QROWS) + j
            out_ref[to, 0:QROWS] = acc[j * QROWS : (j + 1) * QROWS]
            out_ref[to, QROWS : QROWS + STATS] = stats


def man_part(q_all, kv):
    vmem = pl.BlockSpec(memory_space=pltpu.VMEM)
    return pl.pallas_call(
        man_kernel,
        out_shape=jax.ShapeDtypeStruct((PEERS, QROWS + STATS, HD), BF),
        in_specs=[vmem, vmem],
        out_specs=vmem,
        compiler_params=pltpu.CompilerParams(vmem_limit_bytes=32 << 20),
        name="manifest_attention",
    )(q_all, kv)


def join_kernel(place_ref, parts_ref, acc_ref, top_ref, total_ref, out_ref, rows_ref):
    stats = parts_ref[:, QROWS : QROWS + STATS, :].reshape(PEERS * STATS, HD)
    lane = lax.broadcasted_iota(jnp.int32, (QROWS, HD), 1)
    row = lax.broadcasted_iota(jnp.int32, (QROWS, HD), 0)
    pick = jnp.where(lane == row + place_ref[0] * QROWS, 1.0, 0.0).astype(BF)
    s = dot(pick, stats, 1, 1)
    n = PEERS * STATS
    kind = lax.broadcasted_iota(jnp.int32, (QROWS, n), 1) % STATS
    totals = pltpu.roll(s, n - 1, 1) + pltpu.roll(s, n - 2, 1)
    own_top = top_ref[:, 0:1]
    top = jnp.maximum(jnp.max(jnp.where(kind == 0, s, -jnp.inf), axis=1, keepdims=True), own_top)
    factor = jnp.where(kind == 0, jnp.exp(jnp.minimum(s - top, 0.0)), 0.0)
    own_factor = jnp.exp(own_top - top)
    total = jnp.sum(factor * totals, axis=1, keepdims=True) + own_factor * total_ref[:, 0:1]
    acc = own_factor * acc_ref[...]
    for i in range(PEERS):
        acc = acc + factor[:, i * STATS : i * STATS + 1] * parts_ref[i, 0:QROWS].astype(F32)
    rows_ref[...] = acc / total
    for h in range(GROUP):
        rows = rows_ref[pl.ds(h, ROWS, stride=GROUP), :].astype(BF)
        for i in range(CHIPS):
            out_ref[i, :, h * HD : (h + 1) * HD] = rows


def join_part(place, parts, acc, top, total):
    smem = pl.BlockSpec(memory_space=pltpu.SMEM)
    vmem = pl.BlockSpec(memory_space=pltpu.VMEM)
    return pl.pallas_call(
        join_kernel,
        out_shape=jax.ShapeDtypeStruct((CHIPS, ROWS, GROUP * HD), BF),
        in_specs=[smem, vmem, vmem, vmem, vmem],
        out_specs=vmem,
        scratch_shapes=[pltpu.VMEM((QROWS, HD), F32)],
        compiler_params=pltpu.CompilerParams(vmem_limit_bytes=32 << 20),
        name="join_attention",
    )(place, parts, acc, top, total)


def project_kernel(x_ref, w0_ref, w1_ref, out_ref):
    w = jnp.concatenate([w0_ref[...], w1_ref[...]], axis=1)
    out_ref[...] = dot(x_ref[...], w, 1, 0).astype(BF)


def add_kernel(a_ref, out_ref):
    block = (a_ref[0].astype(F32) + a_ref[1].astype(F32)).astype(BF)
    for i in range(4):
        out_ref[i] = block


def mlp_kernel(x_ref, g0_ref, g1_ref, u0_ref, u1_ref, out_ref):
    x = x_ref[...]
    turned = x.astype(F32).reshape(CHIPS // 2, 2 * ROWS, 2 * HD)
    turned = jnp.concatenate([turned[:, ROWS:], turned[:, :ROWS]], axis=1).reshape(CHIPS * ROWS, 2 * HD).astype(BF)
    gate = dot(x, jnp.concatenate([g0_ref[...], g1_ref[...]], axis=0), 1, 0)
    up = dot(turned, jnp.concatenate([u0_ref[...], u1_ref[...]], axis=0), 1, 0)
    low = lax.broadcasted_iota(jnp.int32, (2 * ROWS, gate.shape[1]), 0) < ROWS
    for j in range(CHIPS // 2):
        at = slice(2 * j * ROWS, 2 * (j + 1) * ROWS)
        out_ref[2 * j] = jnp.where(low, gate[at], up[at]).astype(BF)
        out_ref[2 * j + 1] = jnp.where(low, up[at], gate[at]).astype(BF)


def dense(kernel, name, out_shape, *args):
    vmem = pl.BlockSpec(memory_space=pltpu.VMEM)
    return pl.pallas_call(
        kernel,
        out_shape=jax.ShapeDtypeStruct(out_shape, BF),
        in_specs=[vmem] * len(args),
        out_specs=vmem,
        compiler_params=pltpu.CompilerParams(vmem_limit_bytes=40 << 20),
        name=name,
    )(*args)


def swap(x):
    return lax.ppermute(x, "c", [(0, 1), (1, 0)])


def exchange(x, axes):
    return lax.all_to_all(x, axes, 0, 0, tiled=True)


def on_device(queries, new_kv, own_kv, man_kv, pages, own_len, resid, w_out, w_gate, w_up):
    core = lax.axis_index("c")
    tie = lax.optimization_barrier
    width = w_gate.shape[1]
    rows = CHIPS * ROWS
    q = queries.reshape(QROWS, HD)
    q_all = exchange(jnp.broadcast_to(q[None], (PEERS, QROWS, HD)), SPARSE).reshape(PEERS * QROWS, HD)
    kv = lax.all_gather(man_kv.reshape(1, 2, 2 * PAGE, HD), ("p", "c"), axis=0, tiled=True)
    parts = exchange(man_part(q_all, kv), SPARSE)
    own = own_part(pages, own_len, q, new_kv, own_kv.reshape(2, POOL * PAGE, HD))
    parts, own, w_out_c = tie((parts, own, swap(w_out)))
    place = (lax.axis_index(SPARSE) % 4).astype(jnp.int32).reshape(1)
    attn = exchange(join_part(place, parts, *own), PLANE).reshape(rows, GROUP * HD)
    attn, w_gate_c, w_up_c = tie((attn, swap(w_gate), swap(w_up)))

    share = dense(project_kernel, "project", (rows, 2 * HD), attn, w_out, w_out_c)
    shares = lax.all_gather(share, "zh", axis=0)
    shares, resid = tie((shares, resid))
    heads = exchange(dense(add_kernel, "add_shares", (4, rows, 2 * HD), shares), "x")
    res = resid.reshape(CHIPS, 2, ROWS, HD)
    mine = jnp.where(core == 0, res[:, 0], res[:, 1])
    theirs = swap(jnp.where(core == 0, res[:, 1], res[:, 0]))
    res = jnp.concatenate([mine, theirs], axis=-1).reshape(rows, 2 * HD).astype(F32)
    out2 = (res + heads.astype(F32).sum(0)).astype(BF)
    both = dense(mlp_kernel, "gate_up", (CHIPS, 2 * ROWS, width), out2, w_gate, w_gate_c, w_up, w_up_c)
    joined = exchange(both, PLANE).astype(F32).sum(0)
    odd = lax.axis_index("zq") == 1
    gate = jnp.where(odd, joined[ROWS:], joined[:ROWS])
    up = jnp.where(odd, joined[:ROWS], joined[ROWS:])
    hidden = (jax.nn.silu(gate) * up).astype(BF)

    kept = out2[:, :HD].reshape(CHIPS, 1, ROWS, HD)
    given = swap(out2[:, HD:]).reshape(CHIPS, 1, ROWS, HD)
    first = jnp.where(core == 0, kept, given)
    second = jnp.where(core == 0, given, kept)
    resid_out = jnp.concatenate([first, second], axis=1).reshape(CHIPS * 2 * ROWS, HD)
    return (resid_out, hidden)


def solution(mesh):
    fine = Mesh(mesh.devices.reshape(8, 2, 2, 2, 2, 4), ("y", "p", "zq", "c", "zh", "x"))
    in_specs = (
        P(REQ, HEAD),
        P(None, REQ, HEAD),
        P(None, REQ, None, HEAD),
        P(None, REQ, None, HEAD),
        P(REQ, None),
        P(REQ),
        P(None, REQ),
        P(HEAD, REQ),
        P(REQ, HEAD),
        P(REQ, HEAD),
    )
    out_specs = (P(None, REQ), P(REQ, HEAD))
    return jax.shard_map(
        on_device, mesh=fine, in_specs=in_specs, out_specs=out_specs, check_vma=False
    )
```

```python
import jax
import jax.numpy as jnp
from jax import lax
from jax.experimental import pallas as pl
from jax.experimental.pallas import tpu as pltpu
from jax.sharding import Mesh, PartitionSpec as P

HD = 128
PAGE = 64
MAXP = 8
GROUP = 8
ROWS = 4
QROWS = ROWS * GROUP
POOL = 32
CHIPS = 32
PEERS = 16
STATS = 8
SCALE = HD**-0.5
PLANE = ("y", "p", "zq")
SPARSE = ("y", "zq")
HEAD = ("zh", "x")
REQ = ("y", "p", "zq", "c")
BF = jnp.bfloat16
F32 = jnp.float32


def dot(a, b, ca, cb):
    return lax.dot_general(a, b, (((ca,), (cb,)), ((), ())), preferred_element_type=F32)


def own_kernel(pages_ref, len_ref, q_ref, new_ref, own_ref, acc_ref, top_ref, total_ref):
    tokens = POOL * PAGE
    scores = dot(q_ref[...], own_ref[0], 1, 1) * SCALE
    page_of = lax.broadcasted_iota(jnp.int32, (GROUP, tokens), 1) // PAGE
    weights, tops, totals, news = [], [], [], []
    for b in range(ROWS):
        count = jnp.zeros((GROUP, tokens), F32)
        for i in range(MAXP):
            page = jnp.where(i < len_ref[b], pages_ref[b, i], -1)
            count = count + jnp.where(page_of == page, 1.0, 0.0)
        s = jnp.where(count > 0.0, scores[b * GROUP : (b + 1) * GROUP], -jnp.inf)
        q = q_ref[b * GROUP : (b + 1) * GROUP].astype(F32)
        s_new = jnp.sum(q * new_ref[0, b : b + 1].astype(F32), axis=1, keepdims=True) * SCALE
        top = jnp.maximum(jnp.max(s, axis=1, keepdims=True), s_new)
        w = jnp.exp(s - top) * count
        w_new = jnp.exp(s_new - top)
        weights.append(w.astype(BF))
        tops.append(top)
        totals.append(jnp.sum(w, axis=1, keepdims=True) + w_new)
        news.append(w_new.astype(BF).astype(F32) * new_ref[1, b : b + 1].astype(F32))
    acc = dot(jnp.concatenate(weights, axis=0), own_ref[1], 1, 0)
    acc_ref[...] = acc + jnp.concatenate(news, axis=0)
    top_ref[...] = jnp.broadcast_to(jnp.concatenate(tops, axis=0), (QROWS, HD))
    total_ref[...] = jnp.broadcast_to(jnp.concatenate(totals, axis=0), (QROWS, HD))


def own_part(pages, own_len, q, new_kv, own_kv):
    smem = pl.BlockSpec(memory_space=pltpu.SMEM)
    vmem = pl.BlockSpec(memory_space=pltpu.VMEM)
    return pl.pallas_call(
        own_kernel,
        out_shape=[jax.ShapeDtypeStruct((QROWS, HD), F32)] * 3,
        in_specs=[smem, smem, vmem, vmem, vmem],
        out_specs=[vmem] * 3,
        compiler_params=pltpu.CompilerParams(vmem_limit_bytes=32 << 20),
        name="own_attention",
    )(pages, own_len, q, new_kv, own_kv)


def man_kernel(q_ref, kv_ref, out_ref):
    keys = jnp.concatenate([kv_ref[i, 0] for i in range(4)], axis=0)
    values = jnp.concatenate([kv_ref[i, 1] for i in range(4)], axis=0)
    row = lax.broadcasted_iota(jnp.int32, (STATS, HD), 0)
    for chunk in range(PEERS * QROWS // HD):
        s = dot(keys, q_ref[chunk * HD : (chunk + 1) * HD], 1, 1) * SCALE
        top = jnp.max(s, axis=0, keepdims=True).astype(BF).astype(F32)
        w = jnp.exp(s - top)
        total = jnp.sum(w, axis=0, keepdims=True)
        high = total.astype(BF).astype(F32)
        acc = dot(w.astype(BF), values, 0, 0).astype(BF)
        stats = jnp.where(row == 0, top, jnp.where(row == 1, high, jnp.where(row == 2, total - high, 0.0)))
        stats = stats.astype(BF)
        for j in range(HD // QROWS):
            to = chunk * (HD // QROWS) + j
            out_ref[to, 0:QROWS] = acc[j * QROWS : (j + 1) * QROWS]
            out_ref[to, QROWS : QROWS + STATS] = stats


def man_part(q_all, kv):
    vmem = pl.BlockSpec(memory_space=pltpu.VMEM)
    return pl.pallas_call(
        man_kernel,
        out_shape=jax.ShapeDtypeStruct((PEERS, QROWS + STATS, HD), BF),
        in_specs=[vmem, vmem],
        out_specs=vmem,
        compiler_params=pltpu.CompilerParams(vmem_limit_bytes=32 << 20),
        name="manifest_attention",
    )(q_all, kv)


def join_kernel(place_ref, parts_ref, acc_ref, top_ref, total_ref, out_ref, rows_ref):
    stats = parts_ref[:, QROWS : QROWS + STATS, :].reshape(PEERS * STATS, HD)
    lane = lax.broadcasted_iota(jnp.int32, (QROWS, HD), 1)
    row = lax.broadcasted_iota(jnp.int32, (QROWS, HD), 0)
    pick = jnp.where(lane == row + place_ref[0] * QROWS, 1.0, 0.0).astype(BF)
    s = dot(pick, stats, 1, 1)
    n = PEERS * STATS
    kind = lax.broadcasted_iota(jnp.int32, (QROWS, n), 1) % STATS
    totals = pltpu.roll(s, n - 1, 1) + pltpu.roll(s, n - 2, 1)
    own_top = top_ref[:, 0:1]
    top = jnp.maximum(jnp.max(jnp.where(kind == 0, s, -jnp.inf), axis=1, keepdims=True), own_top)
    factor = jnp.where(kind == 0, jnp.exp(jnp.minimum(s - top, 0.0)), 0.0)
    own_factor = jnp.exp(own_top - top)
    total = jnp.sum(factor * totals, axis=1, keepdims=True) + own_factor * total_ref[:, 0:1]
    acc = own_factor * acc_ref[...]
    for i in range(PEERS):
        acc = acc + factor[:, i * STATS : i * STATS + 1] * parts_ref[i, 0:QROWS].astype(F32)
    rows_ref[...] = acc / total
    for h in range(GROUP):
        rows = rows_ref[pl.ds(h, ROWS, stride=GROUP), :].astype(BF)
        for i in range(CHIPS):
            out_ref[i, :, h * HD : (h + 1) * HD] = rows


def join_part(place, parts, acc, top, total):
    smem = pl.BlockSpec(memory_space=pltpu.SMEM)
    vmem = pl.BlockSpec(memory_space=pltpu.VMEM)
    return pl.pallas_call(
        join_kernel,
        out_shape=jax.ShapeDtypeStruct((CHIPS, ROWS, GROUP * HD), BF),
        in_specs=[smem, vmem, vmem, vmem, vmem],
        out_specs=vmem,
        scratch_shapes=[pltpu.VMEM((QROWS, HD), F32)],
        compiler_params=pltpu.CompilerParams(vmem_limit_bytes=32 << 20),
        name="join_attention",
    )(place, parts, acc, top, total)


def project_kernel(x_ref, w0_ref, w1_ref, out_ref):
    w = jnp.concatenate([w0_ref[...], w1_ref[...]], axis=1)
    out_ref[...] = dot(x_ref[...], w, 1, 0).astype(BF)


def add_kernel(a_ref, out_ref):
    block = (a_ref[0].astype(F32) + a_ref[1].astype(F32)).astype(BF)
    for i in range(4):
        out_ref[i] = block


def mlp_kernel(x_ref, g0_ref, g1_ref, u0_ref, u1_ref, out_ref):
    x = x_ref[...]
    turned = x.astype(F32).reshape(CHIPS // 2, 2 * ROWS, 2 * HD)
    turned = jnp.concatenate([turned[:, ROWS:], turned[:, :ROWS]], axis=1).reshape(CHIPS * ROWS, 2 * HD).astype(BF)
    gate = dot(x, jnp.concatenate([g0_ref[...], g1_ref[...]], axis=0), 1, 0)
    up = dot(turned, jnp.concatenate([u0_ref[...], u1_ref[...]], axis=0), 1, 0)
    low = lax.broadcasted_iota(jnp.int32, (2 * ROWS, gate.shape[1]), 0) < ROWS
    for j in range(CHIPS // 2):
        at = slice(2 * j * ROWS, 2 * (j + 1) * ROWS)
        out_ref[2 * j] = jnp.where(low, gate[at], up[at]).astype(BF)
        out_ref[2 * j + 1] = jnp.where(low, up[at], gate[at]).astype(BF)


def dense(kernel, name, out_shape, *args):
    vmem = pl.BlockSpec(memory_space=pltpu.VMEM)
    return pl.pallas_call(
        kernel,
        out_shape=jax.ShapeDtypeStruct(out_shape, BF),
        in_specs=[vmem] * len(args),
        out_specs=vmem,
        compiler_params=pltpu.CompilerParams(vmem_limit_bytes=40 << 20),
        name=name,
    )(*args)


def swap(x):
    return lax.ppermute(x, "c", [(0, 1), (1, 0)])


def exchange(x, axes):
    return lax.all_to_all(x, axes, 0, 0, tiled=True)


def on_device(queries, new_kv, own_kv, man_kv, pages, own_len, resid, w_out, w_gate, w_up):
    core = lax.axis_index("c")
    tie = lax.optimization_barrier
    width = w_gate.shape[1]
    rows = CHIPS * ROWS
    q = queries.reshape(QROWS, HD)
    q_all = exchange(jnp.broadcast_to(queries[None], (PEERS, *queries.shape)), SPARSE).reshape(PEERS * QROWS, HD)
    kv = lax.all_gather(man_kv.reshape(1, 2, 2 * PAGE, HD), ("p", "c"), axis=0, tiled=True)
    parts = exchange(man_part(q_all, kv), SPARSE)
    own = own_part(pages, own_len, q, new_kv, own_kv.reshape(2, POOL * PAGE, HD))
    parts, own, w_out_c = tie((parts, own, swap(w_out)))
    place = (lax.axis_index(SPARSE) % 4).astype(jnp.int32).reshape(1)
    attn = exchange(join_part(place, parts, *own), PLANE).reshape(rows, GROUP * HD)
    attn, w_gate_c, w_up_c = tie((attn, swap(w_gate), swap(w_up)))

    share = dense(project_kernel, "project", (rows, 2 * HD), attn, w_out, w_out_c)
    shares = lax.all_gather(share, "zh", axis=0)
    shares, resid = tie((shares, resid))
    heads = exchange(dense(add_kernel, "add_shares", (4, rows, 2 * HD), shares), "x")
    res = resid.reshape(CHIPS, 2, ROWS, HD)
    mine = jnp.where(core == 0, res[:, 0], res[:, 1])
    theirs = swap(jnp.where(core == 0, res[:, 1], res[:, 0]))
    res = jnp.concatenate([mine, theirs], axis=-1).reshape(rows, 2 * HD).astype(F32)
    out2 = (res + heads.astype(F32).sum(0)).astype(BF)
    both = dense(mlp_kernel, "gate_up", (CHIPS, 2 * ROWS, width), out2, w_gate, w_gate_c, w_up, w_up_c)
    joined = exchange(both, PLANE).astype(F32).sum(0)
    odd = lax.axis_index("zq") == 1
    gate = jnp.where(odd, joined[ROWS:], joined[:ROWS])
    up = jnp.where(odd, joined[:ROWS], joined[ROWS:])
    hidden = (jax.nn.silu(gate) * up).astype(BF)

    kept = out2[:, :HD].reshape(CHIPS, 1, ROWS, HD)
    given = swap(out2[:, HD:]).reshape(CHIPS, 1, ROWS, HD)
    first = jnp.where(core == 0, kept, given)
    second = jnp.where(core == 0, given, kept)
    resid_out = jnp.concatenate([first, second], axis=1).reshape(CHIPS * 2 * ROWS, HD)
    return (resid_out, hidden)


def solution(mesh):
    fine = Mesh(mesh.devices.reshape(8, 2, 2, 2, 2, 4), ("y", "p", "zq", "c", "zh", "x"))
    in_specs = (
        P(REQ, HEAD),
        P(None, REQ, HEAD),
        P(None, REQ, None, HEAD),
        P(None, REQ, None, HEAD),
        P(REQ, None),
        P(REQ),
        P(None, REQ),
        P(HEAD, REQ),
        P(REQ, HEAD),
        P(REQ, HEAD),
    )
    out_specs = (P(None, REQ), P(REQ, HEAD))
    return jax.shard_map(
        on_device, mesh=fine, in_specs=in_specs, out_specs=out_specs, check_vma=False
    )
```

```python
import jax
import jax.numpy as jnp
from jax import lax
from jax.experimental import pallas as pl
from jax.experimental.pallas import tpu as pltpu
from jax.sharding import Mesh, PartitionSpec as P

HD = 128
PAGE = 64
MAXP = 8
GROUP = 8
ROWS = 4
QROWS = ROWS * GROUP
POOL = 32
CHIPS = 32
PEERS = 16
STATS = 8
SCALE = HD**-0.5
PLANE = ("y", "p", "zq")
SPARSE = ("y", "zq")
HEAD = ("zh", "x")
REQ = ("y", "p", "zq", "c")
BF = jnp.bfloat16
F32 = jnp.float32


def dot(a, b, ca, cb):
    return lax.dot_general(a, b, (((ca,), (cb,)), ((), ())), preferred_element_type=F32)


def own_kernel(pages_ref, len_ref, q_ref, new_ref, own_ref, acc_ref, top_ref, total_ref):
    tokens = POOL * PAGE
    scores = dot(q_ref[...], own_ref[0], 1, 1) * SCALE
    page_of = lax.broadcasted_iota(jnp.int32, (GROUP, tokens), 1) // PAGE
    weights, tops, totals, news = [], [], [], []
    for b in range(ROWS):
        count = jnp.zeros((GROUP, tokens), F32)
        for i in range(MAXP):
            page = jnp.where(i < len_ref[b], pages_ref[b, i], -1)
            count = count + jnp.where(page_of == page, 1.0, 0.0)
        s = jnp.where(count > 0.0, scores[b * GROUP : (b + 1) * GROUP], -jnp.inf)
        q = q_ref[b * GROUP : (b + 1) * GROUP].astype(F32)
        s_new = jnp.sum(q * new_ref[0, b : b + 1].astype(F32), axis=1, keepdims=True) * SCALE
        top = jnp.maximum(jnp.max(s, axis=1, keepdims=True), s_new)
        w = jnp.exp(s - top) * count
        w_new = jnp.exp(s_new - top)
        weights.append(w.astype(BF))
        tops.append(top)
        totals.append(jnp.sum(w, axis=1, keepdims=True) + w_new)
        news.append(w_new.astype(BF).astype(F32) * new_ref[1, b : b + 1].astype(F32))
    acc = dot(jnp.concatenate(weights, axis=0), own_ref[1], 1, 0)
    acc_ref[...] = acc + jnp.concatenate(news, axis=0)
    top_ref[...] = jnp.broadcast_to(jnp.concatenate(tops, axis=0), (QROWS, HD))
    total_ref[...] = jnp.broadcast_to(jnp.concatenate(totals, axis=0), (QROWS, HD))


def own_part(pages, own_len, q, new_kv, own_kv):
    smem = pl.BlockSpec(memory_space=pltpu.SMEM)
    vmem = pl.BlockSpec(memory_space=pltpu.VMEM)
    return pl.pallas_call(
        own_kernel,
        out_shape=[jax.ShapeDtypeStruct((QROWS, HD), F32)] * 3,
        in_specs=[smem, smem, vmem, vmem, vmem],
        out_specs=[vmem] * 3,
        compiler_params=pltpu.CompilerParams(vmem_limit_bytes=32 << 20),
        name="own_attention",
    )(pages, own_len, q, new_kv, own_kv)


def man_kernel(q_ref, kv_ref, out_ref):
    keys = jnp.concatenate([kv_ref[i, 0] for i in range(4)], axis=0)
    values = jnp.concatenate([kv_ref[i, 1] for i in range(4)], axis=0)
    row = lax.broadcasted_iota(jnp.int32, (STATS, HD), 0)
    for chunk in range(PEERS * QROWS // HD):
        s = dot(keys, q_ref[chunk * HD : (chunk + 1) * HD], 1, 1) * SCALE
        top = jnp.max(s, axis=0, keepdims=True).astype(BF).astype(F32)
        w = jnp.exp(s - top)
        total = jnp.sum(w, axis=0, keepdims=True)
        high = total.astype(BF).astype(F32)
        acc = dot(w.astype(BF), values, 0, 0).astype(BF)
        stats = jnp.where(row == 0, top, jnp.where(row == 1, high, jnp.where(row == 2, total - high, 0.0)))
        stats = stats.astype(BF)
        for j in range(HD // QROWS):
            to = chunk * (HD // QROWS) + j
            out_ref[to, 0:QROWS] = acc[j * QROWS : (j + 1) * QROWS]
            out_ref[to, QROWS : QROWS + STATS] = stats


def man_part(q_all, kv):
    vmem = pl.BlockSpec(memory_space=pltpu.VMEM)
    return pl.pallas_call(
        man_kernel,
        out_shape=jax.ShapeDtypeStruct((PEERS, QROWS + STATS, HD), BF),
        in_specs=[vmem, vmem],
        out_specs=vmem,
        compiler_params=pltpu.CompilerParams(vmem_limit_bytes=32 << 20),
        name="manifest_attention",
    )(q_all, kv)


def join_kernel(place_ref, parts_ref, acc_ref, top_ref, total_ref, out_ref, rows_ref):
    stats = parts_ref[:, QROWS : QROWS + STATS, :].reshape(PEERS * STATS, HD)
    lane = lax.broadcasted_iota(jnp.int32, (QROWS, HD), 1)
    row = lax.broadcasted_iota(jnp.int32, (QROWS, HD), 0)
    pick = jnp.where(lane == row + place_ref[0] * QROWS, 1.0, 0.0).astype(BF)
    s = dot(pick, stats, 1, 1)
    n = PEERS * STATS
    kind = lax.broadcasted_iota(jnp.int32, (QROWS, n), 1) % STATS
    totals = pltpu.roll(s, n - 1, 1) + pltpu.roll(s, n - 2, 1)
    own_top = top_ref[:, 0:1]
    top = jnp.maximum(jnp.max(jnp.where(kind == 0, s, -jnp.inf), axis=1, keepdims=True), own_top)
    factor = jnp.where(kind == 0, jnp.exp(jnp.minimum(s - top, 0.0)), 0.0)
    own_factor = jnp.exp(own_top - top)
    total = jnp.sum(factor * totals, axis=1, keepdims=True) + own_factor * total_ref[:, 0:1]
    acc = own_factor * acc_ref[...]
    for i in range(PEERS):
        acc = acc + factor[:, i * STATS : i * STATS + 1] * parts_ref[i, 0:QROWS].astype(F32)
    rows_ref[...] = acc / total
    for h in range(GROUP):
        rows = rows_ref[pl.ds(h, ROWS, stride=GROUP), :].astype(BF)
        for i in range(CHIPS):
            out_ref[i, :, h * HD : (h + 1) * HD] = rows


def join_part(place, parts, acc, top, total):
    smem = pl.BlockSpec(memory_space=pltpu.SMEM)
    vmem = pl.BlockSpec(memory_space=pltpu.VMEM)
    return pl.pallas_call(
        join_kernel,
        out_shape=jax.ShapeDtypeStruct((CHIPS, ROWS, GROUP * HD), BF),
        in_specs=[smem, vmem, vmem, vmem, vmem],
        out_specs=vmem,
        scratch_shapes=[pltpu.VMEM((QROWS, HD), F32)],
        compiler_params=pltpu.CompilerParams(vmem_limit_bytes=32 << 20),
        name="join_attention",
    )(place, parts, acc, top, total)


def project_kernel(x_ref, w0_ref, w1_ref, out_ref):
    w = jnp.concatenate([w0_ref[...], w1_ref[...]], axis=1)
    out_ref[...] = dot(x_ref[...], w, 1, 0).astype(BF)


def add_kernel(a_ref, out_ref):
    block = (a_ref[0].astype(F32) + a_ref[1].astype(F32)).astype(BF)
    for i in range(4):
        out_ref[i] = block


def mlp_kernel(x_ref, g0_ref, g1_ref, u0_ref, u1_ref, out_ref):
    x = x_ref[...]
    turned = x.astype(F32).reshape(CHIPS // 2, 2 * ROWS, 2 * HD)
    turned = jnp.concatenate([turned[:, ROWS:], turned[:, :ROWS]], axis=1).reshape(CHIPS * ROWS, 2 * HD).astype(BF)
    gate = dot(x, jnp.concatenate([g0_ref[...], g1_ref[...]], axis=0), 1, 0)
    up = dot(turned, jnp.concatenate([u0_ref[...], u1_ref[...]], axis=0), 1, 0)
    low = lax.broadcasted_iota(jnp.int32, (2 * ROWS, gate.shape[1]), 0) < ROWS
    for j in range(CHIPS // 2):
        at = slice(2 * j * ROWS, 2 * (j + 1) * ROWS)
        out_ref[2 * j] = jnp.where(low, gate[at], up[at]).astype(BF)
        out_ref[2 * j + 1] = jnp.where(low, up[at], gate[at]).astype(BF)


def dense(kernel, name, out_shape, *args):
    vmem = pl.BlockSpec(memory_space=pltpu.VMEM)
    return pl.pallas_call(
        kernel,
        out_shape=jax.ShapeDtypeStruct(out_shape, BF),
        in_specs=[vmem] * len(args),
        out_specs=vmem,
        compiler_params=pltpu.CompilerParams(vmem_limit_bytes=40 << 20),
        name=name,
    )(*args)


def swap(x):
    return lax.ppermute(x, "c", [(0, 1), (1, 0)])


def exchange(x, axes):
    return lax.all_to_all(x, axes, 0, 0, tiled=True)


def on_device(queries, new_kv, own_kv, man_kv, pages, own_len, resid, w_out, w_gate, w_up):
    core = lax.axis_index("c")
    tie = lax.optimization_barrier
    width = w_gate.shape[1]
    rows = CHIPS * ROWS
    q = queries.reshape(QROWS, HD)
    q_all = exchange(jnp.broadcast_to(q[None], (PEERS, QROWS, HD)), SPARSE).reshape(PEERS * QROWS, HD)
    kv = lax.all_gather(man_kv.reshape(1, 2, 2 * PAGE, HD), ("c", "p"), axis=0, tiled=True)
    parts = exchange(man_part(q_all, kv), SPARSE)
    own = own_part(pages, own_len, q, new_kv, own_kv.reshape(2, POOL * PAGE, HD))
    parts, own, w_out_c = tie((parts, own, swap(w_out)))
    place = (lax.axis_index(SPARSE) % 4).astype(jnp.int32).reshape(1)
    attn = exchange(join_part(place, parts, *own), PLANE).reshape(rows, GROUP * HD)
    attn, w_gate_c, w_up_c = tie((attn, swap(w_gate), swap(w_up)))

    share = dense(project_kernel, "project", (rows, 2 * HD), attn, w_out, w_out_c)
    shares = lax.all_gather(share, "zh", axis=0)
    shares, resid = tie((shares, resid))
    heads = exchange(dense(add_kernel, "add_shares", (4, rows, 2 * HD), shares), "x")
    res = resid.reshape(CHIPS, 2, ROWS, HD)
    mine = jnp.where(core == 0, res[:, 0], res[:, 1])
    theirs = swap(jnp.where(core == 0, res[:, 1], res[:, 0]))
    res = jnp.concatenate([mine, theirs], axis=-1).reshape(rows, 2 * HD).astype(F32)
    out2 = (res + heads.astype(F32).sum(0)).astype(BF)
    both = dense(mlp_kernel, "gate_up", (CHIPS, 2 * ROWS, width), out2, w_gate, w_gate_c, w_up, w_up_c)
    joined = exchange(both, PLANE).astype(F32).sum(0)
    odd = lax.axis_index("zq") == 1
    gate = jnp.where(odd, joined[ROWS:], joined[:ROWS])
    up = jnp.where(odd, joined[:ROWS], joined[ROWS:])
    hidden = (jax.nn.silu(gate) * up).astype(BF)

    kept = out2[:, :HD].reshape(CHIPS, 1, ROWS, HD)
    given = swap(out2[:, HD:]).reshape(CHIPS, 1, ROWS, HD)
    first = jnp.where(core == 0, kept, given)
    second = jnp.where(core == 0, given, kept)
    resid_out = jnp.concatenate([first, second], axis=1).reshape(CHIPS * 2 * ROWS, HD)
    return (resid_out, hidden)


def solution(mesh):
    fine = Mesh(mesh.devices.reshape(8, 2, 2, 2, 2, 4), ("y", "p", "zq", "c", "zh", "x"))
    in_specs = (
        P(REQ, HEAD),
        P(None, REQ, HEAD),
        P(None, REQ, None, HEAD),
        P(None, REQ, None, HEAD),
        P(REQ, None),
        P(REQ),
        P(None, REQ),
        P(HEAD, REQ),
        P(REQ, HEAD),
        P(REQ, HEAD),
    )
    out_specs = (P(None, REQ), P(REQ, HEAD))
    return jax.shard_map(
        on_device, mesh=fine, in_specs=in_specs, out_specs=out_specs, check_vma=False
    )
```
